32 devices in a mesh: dp: 8 (over z, x), tensor: 4 (over y, core).
Axes of the slice: x: 2, y: 2, z: 4, core: 2. Of those that a mesh axis runs over, the one named last changes fastest.
Arguments:
- hidden_in: float32 [4096, 1536], P('dp'), may hold values from -6 to 6
- doc_lengths: int32 [2, 2], replicated, may hold values from 1 to 1792, 2048 in all within a row
- norm_attn: float32 [2, 1536], replicated, may hold values from 0.5 to 1.5
- norm_mlp: float32 [2, 1536], replicated, may hold values from 0.5 to 1.5
- w_query: bfloat16 [2, 1536, 1536], P(None, None, 'tensor'), may hold values from -0.15625 to 0.15625
- w_key: bfloat16 [2, 1536, 768], P(None, None, 'tensor'), may hold values from -0.15625 to 0.15625
- w_value: bfloat16 [2, 1536, 768], P(None, None, 'tensor'), may hold values from -0.15625 to 0.15625
- w_out: bfloat16 [2, 1536, 1536], P(None, 'tensor'), may hold values from -0.625 to 0.625
- w_gate: bfloat16 [2, 1536, 4096], P(None, None, 'tensor'), may hold values from -0.15625 to 0.15625
- w_up: bfloat16 [2, 1536, 4096], P(None, None, 'tensor'), may hold values from -0.15625 to 0.15625
- w_down: bfloat16 [2, 4096, 1536], P(None, 'tensor'), may hold values from -0.09375 to 0.09375
- cotangent: float32 [4096, 1536], P('dp'), may hold values from -6 to 6
Outputs:
- hidden_out: float32 [4096, 1536], P('dp')
- input_grad: float32 [4096, 1536], P('dp')
- norm_attn_grad: float32 [2, 1536], P(None, 'dp')
- norm_mlp_grad: float32 [2, 1536], P(None, 'dp')
- w_query_grad: float32 [2, 1536, 1536], P(None, 'dp', 'tensor')
- w_key_grad: float32 [2, 1536, 768], P(None, 'dp', 'tensor')
- w_value_grad: float32 [2, 1536, 768], P(None, 'dp', 'tensor')
- w_out_grad: float32 [2, 1536, 1536], P(None, 'tensor', 'dp')
- w_gate_grad: float32 [2, 1536, 4096], P(None, 'dp', 'tensor')
- w_up_grad: float32 [2, 1536, 4096], P(None, 'dp', 'tensor')
- w_down_grad: float32 [2, 4096, 1536], P(None, 'tensor', 'dp')
The draws below stay inside these ranges and needn't reach their ends.
Inputs may be any that keep to these rules, and one draw needn't show every extreme that they name: `doc_lengths`: each row holds 2 document lengths that add up to 2048, each at most 1792.
All inputs are finite; a program needn't handle non-finite values.
Results may differ from the reference program's by a relative error of at most 0.028.
Values may be sent and summed in bfloat16 or wider, within the bound.
No kernel may reach another device: no remote copies, remote signals or barrier semaphores. Data moves between devices by JAX's collectives and lax.ppermute only.
A program may use at most 320 MiB of HBM per device.

```python
import math
import jax
import jax.numpy as jnp
import numpy as np
from jax import lax

D = 1536
H = 16
KV = 8
HD = 96
FF = 4096
LAYERS = 2
DOCS = 2
TOK_DEV = 512
SEQ_LEN = 2048
SEQS = 2
TOKENS = 4096


def raised(drawn, key, source, target, shards_of, factor):
    def block_of(axis_at):
        return (jnp.arange(drawn.shape[axis_at]) // (drawn.shape[axis_at] // shards_of)).reshape((-1,) + (1,) * (drawn.ndim - 1 - axis_at))

    one_side = jax.random.permutation(key, shards_of)[block_of(target)]
    other_side = (block_of(target) + shards_of // 2) % shards_of
    return jnp.where((block_of(source) == one_side) | (block_of(source) == other_side), factor * drawn, drawn)


def shard_levels(own_key, dims, cuts, least, high):
    factor_of = 1.0
    for dim, parts in cuts:
        heights = jax.random.uniform(jax.random.fold_in(jax.random.fold_in(own_key, 6), dim), (parts,), jnp.float32, least / len(cuts), high / len(cuts))
        factor_of = factor_of * jnp.repeat(jnp.exp(heights), dims[dim] // parts).reshape((-1,) + (1,) * (len(dims) - 1 - dim))
    return factor_of


def profile(amount, total, reach, slope):
    weights = [(1 << 20) // math.isqrt(grade ** slope) + 1 for grade in range(2, amount + 1)]
    rest, given = total - reach - (amount - 1), [1] * (amount - 1)
    while rest > 0:
        movable = [i for i in range(amount - 1) if given[i] < reach]
        pool, budget = sum([weights[i] for i in movable]), rest
        for i in movable:
            more = min(reach - given[i], max(1, budget * weights[i] // pool), rest)
            given[i] = given[i] + more
            rest = rest - more
    return np.array([reach] + given)


def ragged_sizes(rng, count, total, bound, slope):
    if count == 2:
        one = jax.random.randint(rng, (), max(1, total - bound), min(bound, total - 1) + 1)
        return jnp.stack([one, total - one])
    sizes = jnp.asarray(profile(count, total, bound, slope), jnp.int32)
    couples = (count - 1) // 2
    giver, receiver = sizes[1:1 + 2 * couples:2], sizes[2:2 + 2 * couples:2]
    slack = jnp.minimum(giver - 1, bound - receiver)
    moved = jax.random.randint(jax.random.fold_in(rng, 1), (couples,), 0, 1 << 20) % (slack + 1)
    sizes = sizes.at[1:1 + 2 * couples:2].set(giver - moved).at[2:2 + 2 * couples:2].set(receiver + moved)
    return sizes[jax.random.permutation(jax.random.fold_in(rng, 2), count)]


def scatter_about(rng, dims, spread, bound, split=(), held_as=jnp.bfloat16):
    entries = jax.random.normal(rng, dims, jnp.float32) * spread
    if len(split) > 0:
        entries = shard_levels(rng, dims, split, -0.22, 0.18) * entries
    return jnp.clip(entries, min=-bound, max=bound).astype(held_as)


def gaussian_with(rng, dims, width, limit, cuts, heavy, kind=jnp.bfloat16):
    array = width * jax.random.normal(rng, dims, jnp.float32)
    if cuts:
        array = array * shard_levels(rng, dims, cuts, -0.22, 0.18)
    return jnp.clip(raised(array, jax.random.fold_in(rng, 3), *heavy), -limit, limit).astype(kind)


def setup_inputs(seed: int = 0) -> dict:
    splits = jax.random.split(jax.random.key(seed), 13)
    return {
        "hidden_in": gaussian_with(splits[0], (TOKENS, D), 1.0, 6.0, ((0, 8),), (0, 1, 8, 2.0), jnp.float32),
        "doc_lengths": jax.vmap(lambda own: ragged_sizes(own, DOCS, SEQ_LEN, SEQ_LEN - TOK_DEV // 2, 2))(jax.random.split(splits[1], SEQS)).reshape((SEQS, DOCS)).astype(jnp.int32),
        "norm_attn": jnp.clip(1.0 + 0.1 * jax.random.normal(splits[2], (LAYERS, D), jnp.float32), 0.5, 1.5),
        "norm_mlp": jnp.clip(1.0 + 0.1 * jax.random.normal(splits[3], (LAYERS, D), jnp.float32), 0.5, 1.5),
        "w_query": scatter_about(splits[4], (LAYERS, D, H * HD), D ** -0.5, 0.15625, ((2, 4),)),
        "w_key": scatter_about(splits[5], (LAYERS, D, KV * HD), D ** -0.5, 0.15625, ((2, 4),)),
        "w_value": scatter_about(splits[6], (LAYERS, D, KV * HD), D ** -0.5, 0.15625, ((2, 4),)),
        "w_out": scatter_about(splits[7], (LAYERS, H * HD, D), HD ** -0.5, 0.625, ((1, 4),)),
        "w_gate": scatter_about(splits[8], (LAYERS, D, FF), D ** -0.5, 0.15625, ((2, 4),)),
        "w_up": scatter_about(splits[9], (LAYERS, D, FF), D ** -0.5, 0.15625, ((2, 4),)),
        "w_down": scatter_about(splits[10], (LAYERS, FF, D), FF ** -0.5, 0.09375, ((1, 4),)),
        "cotangent": gaussian_with(splits[11], (TOKENS, D), 1.0, 6.0, ((0, 8),), (0, 1, 8, 2.0), jnp.float32),
    }


EPS = 1e-05
BASE = 100000.0

def rope_tables(positions):
    half_dim = HD // 2
    frequency = BASE ** (-(jnp.arange(half_dim, dtype=jnp.float32) * 2.0 / HD))
    angles = positions.astype(jnp.float32)[:, None] * frequency[None, :]
    angles = jnp.concatenate([angles, angles], axis=1)
    return (jnp.cos(angles)[:, None, :], jnp.sin(angles)[:, None, :])

def rotate(values, cosine, sine_table):
    half_dim = values.shape[-1] // 2
    turned = jnp.concatenate([-values[..., half_dim:], values[..., :half_dim]], axis=-1)
    return values * cosine + turned * sine_table

def unrotate(gradient, cosine, sine_table):
    half_dim = gradient.shape[-1] // 2
    scaled_values = gradient * sine_table
    turned = jnp.concatenate([scaled_values[..., half_dim:], -scaled_values[..., :half_dim]], axis=-1)
    return gradient * cosine + turned

def doc_place(places, lengths):
    doc_ends = jnp.cumsum(lengths, axis=1).astype(jnp.int32)
    passed = (places[:, None] >= doc_ends).astype(jnp.int32)
    doc_ids = lax.optimization_barrier(jnp.sum(passed, axis=1)).astype(jnp.int32)
    starts = lax.optimization_barrier(jnp.sum(passed * lengths, axis=1)).astype(jnp.int32)
    return (doc_ids, (places - starts).astype(jnp.int32))

def scores_of(queries, key_rows, allowed):
    scores = jnp.einsum('qkgd,tkd->kgqt', queries.astype(jnp.float32), key_rows.astype(jnp.float32)) * HD ** (-0.5)
    return jnp.where(allowed[None, None], scores, -jnp.inf)

def attention_forward(queries, key_rows, value_rows, allowed):
    scores = scores_of(queries, key_rows, allowed)
    row_top = lax.optimization_barrier(jnp.max(scores, axis=-1, keepdims=True))
    log_total = row_top + jnp.log(lax.optimization_barrier(jnp.sum(jnp.exp(scores - row_top), axis=-1, keepdims=True)))
    attn_probs = jnp.exp(scores - log_total).astype(jnp.bfloat16)
    mixed_heads = jnp.einsum('kgqt,tkd->qkgd', attn_probs.astype(jnp.float32), value_rows.astype(jnp.float32))
    return (mixed_heads.astype(jnp.bfloat16), log_total)

def attention_backward(queries, key_rows, value_rows, allowed, log_total, mixed_grad):
    scores = scores_of(queries, key_rows, allowed)
    attn_probs = jnp.exp(scores - log_total)
    grad_f = mixed_grad.astype(jnp.float32)
    prob_grad = jnp.einsum('qkgd,tkd->kgqt', grad_f, value_rows.astype(jnp.float32))
    centre = lax.optimization_barrier(jnp.sum(attn_probs * prob_grad, axis=-1, keepdims=True))
    score_grad = (attn_probs * (prob_grad - centre) * HD ** (-0.5)).astype(jnp.bfloat16).astype(jnp.float32)
    probs_bf = attn_probs.astype(jnp.bfloat16).astype(jnp.float32)
    value_grad = jnp.einsum('kgqt,qkgd->tkd', probs_bf, grad_f)
    query_grad = jnp.einsum('kgqt,tkd->qkgd', score_grad, key_rows.astype(jnp.float32))
    key_grad = jnp.einsum('kgqt,qkgd->tkd', score_grad, queries.astype(jnp.float32))
    return (query_grad, key_grad, value_grad)

def causal_mask(doc_ids):
    places = jnp.arange(doc_ids.shape[0], dtype=jnp.int32)
    return (places[None, :] <= places[:, None]) & (doc_ids[None, :] == doc_ids[:, None])

def norm_back(residual_stream, inverse_norm, gain, normalized_gradient, incoming_gradient):
    normalized_input = residual_stream * inverse_norm
    scaled_values = normalized_gradient * gain
    gain_gradient = lax.optimization_barrier(jnp.sum(normalized_gradient * normalized_input, axis=0))
    residual_gradient = incoming_gradient + inverse_norm * (scaled_values - normalized_input * lax.optimization_barrier(jnp.mean(scaled_values * normalized_input, axis=1, keepdims=True)))
    return (residual_gradient, gain_gradient)

def forward_layer(residual_stream, params, tables, doc_seq):
    gain_attn, gain_mlp, query_w, key_w, value_w, out_w, gate_w, up_w, down_w = params
    cosine, sine_table = tables
    row_count = residual_stream.shape[0]
    seq_count = row_count // SEQ_LEN
    group = H // KV
    inv_attn = lax.rsqrt(lax.optimization_barrier(jnp.mean(residual_stream * residual_stream, axis=1, keepdims=True)) + EPS)
    normed_attn = (residual_stream * inv_attn * gain_attn).astype(jnp.bfloat16)
    queries = jnp.dot(normed_attn, query_w, preferred_element_type=jnp.float32).reshape(row_count, H, HD)
    queries = rotate(queries, cosine, sine_table).astype(jnp.bfloat16)
    key_rows = jnp.dot(normed_attn, key_w, preferred_element_type=jnp.float32).reshape(row_count, KV, HD)
    key_rows = rotate(key_rows, cosine, sine_table).astype(jnp.bfloat16)
    value_rows = jnp.dot(normed_attn, value_w, preferred_element_type=jnp.float32).astype(jnp.bfloat16).reshape(row_count, KV, HD)
    grouped = queries.reshape(seq_count, SEQ_LEN, KV, group, HD)
    key_seq = key_rows.reshape(seq_count, SEQ_LEN, KV, HD)
    value_seq = value_rows.reshape(seq_count, SEQ_LEN, KV, HD)

    def one_sequence(members):
        return attention_forward(members[0], members[1], members[2], causal_mask(members[3]))
    mixed_heads, log_total = lax.map(one_sequence, (grouped, key_seq, value_seq, doc_seq))
    mixed_heads = mixed_heads.reshape(row_count, H * HD)
    middle = residual_stream + jnp.dot(mixed_heads, out_w, preferred_element_type=jnp.float32)
    inv_mlp = lax.rsqrt(lax.optimization_barrier(jnp.mean(middle * middle, axis=1, keepdims=True)) + EPS)
    normed_mlp = (middle * inv_mlp * gain_mlp).astype(jnp.bfloat16)
    gate_pre = jnp.dot(normed_mlp, gate_w, preferred_element_type=jnp.float32)
    up_values = jnp.dot(normed_mlp, up_w, preferred_element_type=jnp.float32)
    activated = (jax.nn.silu(gate_pre) * up_values).astype(jnp.bfloat16)
    result = middle + jnp.dot(activated, down_w, preferred_element_type=jnp.float32)
    record = (residual_stream, inv_attn, normed_attn, grouped, key_seq, value_seq, log_total, mixed_heads, middle, inv_mlp, normed_mlp, gate_pre, up_values, activated)
    return (record, result)

def backward_layer(grad_flow, record, params, tables, doc_seq):
    gain_attn, gain_mlp, query_w, key_w, value_w, out_w, gate_w, up_w, down_w = params
    residual_stream, inv_attn, normed_attn, grouped, key_seq, value_seq, log_total, mixed_heads, middle, inv_mlp, normed_mlp, gate_pre, up_values, activated = record
    cosine, sine_table = tables
    row_count = residual_stream.shape[0]
    group = H // KV
    down_in = grad_flow.astype(jnp.bfloat16)
    grad_down = jnp.dot(activated.T, down_in, preferred_element_type=jnp.float32)
    hidden_grad = jnp.dot(down_in, down_w.T, preferred_element_type=jnp.float32)
    sigmoid_gate = jax.nn.sigmoid(gate_pre)
    gate_grad = (hidden_grad * up_values * sigmoid_gate * (1.0 + gate_pre * (1.0 - sigmoid_gate))).astype(jnp.bfloat16)
    up_grad = (hidden_grad * gate_pre * sigmoid_gate).astype(jnp.bfloat16)
    grad_gate = jnp.dot(normed_mlp.T, gate_grad, preferred_element_type=jnp.float32)
    grad_up = jnp.dot(normed_mlp.T, up_grad, preferred_element_type=jnp.float32)
    mlp_norm_grad = jnp.dot(gate_grad, gate_w.T, preferred_element_type=jnp.float32) + jnp.dot(up_grad, up_w.T, preferred_element_type=jnp.float32)
    middle_grad, grad_gain_mlp = norm_back(middle, inv_mlp, gain_mlp, mlp_norm_grad, grad_flow)
    out_in = middle_grad.astype(jnp.bfloat16)
    grad_out = jnp.dot(mixed_heads.T, out_in, preferred_element_type=jnp.float32)
    mixed_grad = jnp.dot(out_in, out_w.T, preferred_element_type=jnp.float32).astype(jnp.bfloat16)
    mixed_grad = mixed_grad.reshape(row_count // SEQ_LEN, SEQ_LEN, KV, group, HD)
    log_seq = log_total

    def one_sequence(members):
        return attention_backward(members[0], members[1], members[2], causal_mask(members[3]), members[4], members[5])
    query_grad, key_grad, value_grad = lax.map(one_sequence, (grouped, key_seq, value_seq, doc_seq, log_seq, mixed_grad))
    query_grad = unrotate(query_grad.reshape(row_count, H, HD), cosine, sine_table).astype(jnp.bfloat16).reshape(row_count, H * HD)
    key_grad = unrotate(key_grad.reshape(row_count, KV, HD), cosine, sine_table).astype(jnp.bfloat16).reshape(row_count, KV * HD)
    value_grad = value_grad.reshape(row_count, KV * HD).astype(jnp.bfloat16)
    grad_query = jnp.dot(normed_attn.T, query_grad, preferred_element_type=jnp.float32)
    grad_key = jnp.dot(normed_attn.T, key_grad, preferred_element_type=jnp.float32)
    grad_value = jnp.dot(normed_attn.T, value_grad, preferred_element_type=jnp.float32)
    attn_norm_grad = jnp.dot(query_grad, query_w.T, preferred_element_type=jnp.float32)
    attn_norm_grad = attn_norm_grad + jnp.dot(key_grad, key_w.T, preferred_element_type=jnp.float32)
    attn_norm_grad = attn_norm_grad + jnp.dot(value_grad, value_w.T, preferred_element_type=jnp.float32)
    residual_gradient, grad_gain_attn = norm_back(residual_stream, inv_attn, gain_attn, attn_norm_grad, middle_grad)
    return (residual_gradient, (grad_gain_attn, grad_gain_mlp, grad_query, grad_key, grad_value, grad_out, grad_gate, grad_up, grad_down))

def reference(hidden_in, doc_lengths, norm_attn, norm_mlp, w_query, w_key, w_value, w_out, w_gate, w_up, w_down, cotangent):
    offset = SEQ_LEN // 2
    row_count = hidden_in.shape[0]
    token_index = jnp.arange(row_count, dtype=jnp.int32)
    places = (token_index % SEQ_LEN).astype(jnp.int32)
    seq_index = (token_index // SEQ_LEN).astype(jnp.int32)
    row_lengths = doc_lengths[seq_index]
    doc_ids, positions = doc_place(places, row_lengths)
    doc_seq = doc_ids.reshape(row_count // SEQ_LEN, SEQ_LEN)
    tables = rope_tables(positions)
    records = []
    flowing = jnp.roll(hidden_in, offset, axis=0)
    for layer_index in range(LAYERS):
        params = (norm_attn[layer_index], norm_mlp[layer_index], w_query[layer_index], w_key[layer_index], w_value[layer_index], w_out[layer_index], w_gate[layer_index], w_up[layer_index], w_down[layer_index])
        record, flowing = forward_layer(flowing, params, tables, doc_seq)
        records.append(record)
    hidden_out = jnp.roll(flowing, -offset, axis=0)
    grad_flow = jnp.roll(cotangent, offset, axis=0)
    collected = [None] * LAYERS
    for layer_index in reversed(range(LAYERS)):
        params = (norm_attn[layer_index], norm_mlp[layer_index], w_query[layer_index], w_key[layer_index], w_value[layer_index], w_out[layer_index], w_gate[layer_index], w_up[layer_index], w_down[layer_index])
        grad_flow, layer_grads = backward_layer(grad_flow, records[layer_index], params, tables, doc_seq)
        collected[layer_index] = layer_grads
    input_grad = jnp.roll(grad_flow, -offset, axis=0)
    stacked = [jnp.stack([member[position] for member in collected]) for position in range(9)]
    return (hidden_out, input_grad, stacked[0], stacked[1], stacked[2], stacked[3], stacked[4], stacked[5], stacked[6], stacked[7], stacked[8])
```

```python
import functools

import jax
import jax.numpy as jnp
from jax import lax
from jax.experimental import pallas as pl
from jax.experimental.pallas import tpu as pltpu
from jax.sharding import PartitionSpec as P

HD = 96
LAYERS = 2
STRETCHES = 4
EPS = 1e-05
BASE = 100000.0

BF = jnp.bfloat16
F32 = jnp.float32
NEG = -1e30
VMEM_BYTES = 56 * 2**20


def mm(a, b, ca, cb):
    return lax.dot_general(a, b, (((ca,), (cb,)), ((), ())), preferred_element_type=F32)


def swap(block, axis, mask):
    n = lax.axis_size(axis)
    return lax.ppermute(block, axis, [(i, i ^ mask) for i in range(n)])


def bf16_of(x):
    return lax.reduce_precision(x, 8, 7).astype(BF)


def gather_rows(own):
    pair = jnp.concatenate([own, swap(own, "tensor", 2)], axis=0)
    return jnp.concatenate([pair, swap(pair, "tensor", 1)], axis=0)


def reduce_rows(keep, send):
    quarter = keep.shape[0] // 2
    got = swap(send, "tensor", 1)
    far = (keep[quarter:] + got[quarter:].astype(F32)).astype(BF)
    near = keep[:quarter] + got[:quarter].astype(F32)
    return near + swap(far, "tensor", 2).astype(F32)


RELATIVE = (0, 2, 1, 3)


def to_relative(rows, index):
    quarter = rows.shape[0] // 4
    return jnp.concatenate(
        [lax.dynamic_slice_in_dim(rows, (index ^ m) * quarter, quarter, 0) for m in RELATIVE], axis=0
    )


def to_absolute(rows, index):
    quarter = rows.shape[0] // 4
    parts = []
    for j in range(4):
        m = index ^ j
        place = ((m & 1) << 1) | (m >> 1)
        parts.append(lax.dynamic_slice_in_dim(rows, place * quarter, quarter, 0))
    return jnp.concatenate(parts, axis=0)


def in_stretches(pairs_of, n):
    pairs = []
    for i in range(n):
        offset = pairs_of((i + STRETCHES // 2) % STRETCHES)
        if offset is not None:
            pairs.append((i, (i + offset) % n))
    return pairs


def keys_onward(kv):
    n = lax.axis_size("dp")
    beside = swap(kv, "dp", 1)
    behind = lax.ppermute(kv, "dp", in_stretches(lambda s: 2 if s < 2 else None, n))
    across = lax.ppermute(behind, "dp", [(i, i ^ 1) for i in range(n) if (i + 2) % 4 >= 2])
    return beside, behind, across


def keys_back(beside, behind, across):
    n = lax.axis_size("dp")
    late = [i for i in range(n) if (i + 2) % 4 >= 2]
    got = lax.ppermute(across, "dp", [(i, i ^ 1) for i in late])
    from_beside = swap(beside, "dp", 1)
    total = (behind.astype(F32) + got.astype(F32)).astype(BF)
    from_behind = lax.ppermute(total, "dp", in_stretches(lambda s: -2 if s >= 2 else None, n))
    return from_beside, from_behind


def scatter_line(grad):
    n = lax.axis_size("dp")
    outer = n // 8
    r = grad.shape[0] * 2 // n
    z = lax.axis_index("dp") // 2 % 4
    g4 = grad.reshape(outer, 4, r, grad.shape[1])
    out_in, middle, in_out = [], [], []
    for i in range(n):
        zi = i // 2 % 4
        if zi in (0, 3):
            j = i + 2 if zi == 0 else i - 2
            out_in.append((i, j))
            in_out.append((j, i))
        else:
            middle.append((i, i + 2 if zi == 1 else i - 2))
    cross = lax.dynamic_slice_in_dim(g4, 2 * (1 - z // 2), 2, 1)
    beside = lax.dynamic_slice_in_dim(g4, z ^ 1, 1, 1)
    got_cross = lax.ppermute(cross, "dp", out_in)
    got_beside = lax.ppermute(beside, "dp", out_in)
    over = lax.ppermute((cross.astype(F32) + got_cross.astype(F32)).astype(BF), "dp", middle)
    on = beside.astype(F32) + lax.dynamic_slice_in_dim(over, (z ^ 1) & 1, 1, 1).astype(F32)
    last = lax.ppermute(on.astype(BF), "dp", in_out)
    own = lax.dynamic_slice_in_dim(g4, z, 1, 1).astype(F32)
    own = own + got_beside.astype(F32)
    own = own + lax.dynamic_slice_in_dim(over, z & 1, 1, 1).astype(F32) + last.astype(F32)
    own = own[:, 0]
    if outer == 1:
        return own[0]
    place = lax.axis_index("dp") // 8
    total = lax.dynamic_index_in_dim(own, place, 0, keepdims=False)
    for k in range(1, outer):
        piece = lax.dynamic_index_in_dim(own, (place + k) % outer, 0, keepdims=False).astype(BF)
        total = total + lax.ppermute(piece, "dp", [(i, (i + 8 * k) % n) for i in range(n)]).astype(F32)
    return total


def sum_everywhere(x):
    x = x + swap(x, "tensor", 1)
    x = x + swap(x, "tensor", 2)
    n = lax.axis_size("dp")
    mask = 1
    while mask < n:
        x = x + swap(x, "dp", mask)
        mask *= 2
    return x


def turned_pair(top, low, cosine, sine):
    return top * cosine - low * sine, low * cosine + top * sine


def qkv_kernel(heads, x_ref, w_ref, cos_ref, sin_ref, out_ref, t_ref):
    t_ref[...] = mm(x_ref[...], w_ref[...], 1, 0).T
    half = HD // 2
    cosine, sine = cos_ref[...], sin_ref[...]
    for h in range(heads):
        a = h * HD
        top, low = turned_pair(t_ref[a : a + half], t_ref[a + half : a + HD], cosine, sine)
        out_ref[a : a + half] = top.astype(BF)
        out_ref[a + half : a + HD] = low.astype(BF)
    rest = heads * HD
    out_ref[rest:] = t_ref[rest:].astype(BF)


def qkv_call(x, w, cosine, sine, heads):
    rows, cols = x.shape[0], w.shape[1]
    return pl.pallas_call(
        functools.partial(qkv_kernel, heads),
        out_shape=jax.ShapeDtypeStruct((cols, rows), BF),
        scratch_shapes=[pltpu.VMEM((cols, rows), F32)],
        compiler_params=pltpu.CompilerParams(vmem_limit_bytes=VMEM_BYTES),
        name="qkv_rotary",
    )(x, w, cosine, sine)


def both_heads(block):
    return jnp.concatenate([block[:HD], block[HD:]], axis=1)


def flip(block):
    return block.astype(F32).T.astype(BF)


def allowed_of(base, rows_ref, top_ref, start_ref):
    key_place = rows_ref[...] + base
    two = lambda ref: jnp.concatenate([ref[...], ref[...]], axis=1)
    return (key_place >= two(start_ref)) & (key_place <= two(top_ref))


def attn_fwd_kernel(base_ref, rows_ref, top_ref, start_ref, q_ref, *refs):
    keys, values = refs[0:8:2], refs[1:8:2]
    mixed_t_ref, log_ref, s_ref = refs[8:]
    qt = both_heads(q_ref[...])
    top = jnp.full((1, qt.shape[1]), NEG, F32)
    for b in range(4):
        scores = mm(flip(keys[b][...]), qt, 1, 0) * HD ** (-0.5)
        scores = jnp.where(allowed_of(base_ref[b], rows_ref, top_ref, start_ref), scores, NEG)
        s_ref[b] = scores
        top = jnp.maximum(top, jnp.max(scores, axis=0, keepdims=True))
    total = jnp.zeros_like(top)
    acc = jnp.zeros((HD, qt.shape[1]), F32)
    for b in range(4):
        weight = jnp.exp(s_ref[b] - top)
        total = total + jnp.sum(weight, axis=0, keepdims=True)
        acc = acc + mm(values[b][...], weight.astype(BF), 1, 0)
    acc = acc / total
    log_ref[0] = top + jnp.log(total)
    half = qt.shape[1] // 2
    mixed_t_ref[:HD] = acc[:, :half].astype(BF)
    mixed_t_ref[HD:] = acc[:, half:].astype(BF)


def attn_specs(rows, kv):
    q_spec = pl.BlockSpec((2 * HD, rows), lambda g: (g, 0))
    own_k = pl.BlockSpec((HD, rows), lambda g: (2 * kv + g, 0))
    own_v = pl.BlockSpec((HD, rows), lambda g: (3 * kv + g, 0))
    far_k = pl.BlockSpec((HD, rows), lambda g: (g, 0))
    far_v = pl.BlockSpec((HD, rows), lambda g: (kv + g, 0))
    whole = lambda shape: pl.BlockSpec(shape, lambda g: (0,) * len(shape))
    places = [
        pl.BlockSpec(memory_space=pltpu.SMEM),
        whole((rows, 1)),
        whole((1, rows)),
        whole((1, rows)),
    ]
    return places, q_spec, [own_k, own_v] + [far_k, far_v] * 3


def attn_fwd(qkv_t, far, places, kv):
    rows = qkv_t.shape[1]
    place_specs, q_spec, kv_specs = attn_specs(rows, kv)
    operands = [qkv_t, qkv_t]
    for block in far:
        operands += [block, block]
    mixed_t, log_total = pl.pallas_call(
        attn_fwd_kernel,
        grid=(kv,),
        in_specs=place_specs + [q_spec] + kv_specs,
        out_specs=[
            pl.BlockSpec((2 * HD, rows), lambda g: (g, 0)),
            pl.BlockSpec((1, 1, 2 * rows), lambda g: (g, 0, 0)),
        ],
        out_shape=[
            jax.ShapeDtypeStruct((2 * kv * HD, rows), BF),
            jax.ShapeDtypeStruct((kv, 1, 2 * rows), F32),
        ],
        scratch_shapes=[pltpu.VMEM((4, rows, 2 * rows), F32)],
        compiler_params=pltpu.CompilerParams(vmem_limit_bytes=VMEM_BYTES),
        name="attention_forward",
    )(*places, qkv_t, *operands)
    return mixed_t, log_total


def attn_bwd_kernel(base_ref, rows_ref, top_ref, start_ref, cos_ref, sin_ref, q_ref, *refs):
    keys, values = refs[0:8:2], refs[1:8:2]
    log_ref, mixed_ref, grad_ref = refs[8:11]
    dq_ref, own_ref, far_refs = refs[11], refs[12], refs[13:]
    qt = both_heads(q_ref[...])
    grad_t = both_heads(grad_ref[...])
    q_rows, grad_rows = flip(qt), flip(grad_t)
    log_total = log_ref[0]
    centre = jnp.sum(
        grad_t.astype(F32) * both_heads(mixed_ref[...]).astype(F32), axis=0, keepdims=True
    )
    dq = jnp.zeros((HD, qt.shape[1]), F32)
    for b in range(4):
        scores = mm(flip(keys[b][...]), qt, 1, 0) * HD ** (-0.5)
        scores = jnp.where(allowed_of(base_ref[b], rows_ref, top_ref, start_ref), scores, NEG)
        probs = jnp.exp(scores - log_total)
        prob_grad = mm(flip(values[b][...]), grad_t, 1, 0)
        score_grad = (probs * (prob_grad - centre) * HD ** (-0.5)).astype(BF)
        dq = dq + mm(keys[b][...], score_grad, 1, 0)
        dv = mm(probs.astype(BF), grad_rows, 1, 0).T
        dk = mm(score_grad, q_rows, 1, 0).T
        out = own_ref if b == 0 else far_refs[b - 1]
        out[0] = dk.astype(out.dtype)
        out[1] = dv.astype(out.dtype)
    half, rows = HD // 2, qt.shape[1] // 2
    cosine, sine = cos_ref[...], sin_ref[...]
    for h in range(2):
        part = dq[:, h * rows : (h + 1) * rows]
        top, low = turned_pair(part[:half], part[half:], cosine, -sine)
        dq_ref[h * HD : h * HD + half] = top.astype(BF)
        dq_ref[h * HD + half : (h + 1) * HD] = low.astype(BF)


def attn_bwd(qkv_t, far, places, kv, tables, log_total, mixed_t, grad_t):
    rows = qkv_t.shape[1]
    place_specs, q_spec, kv_specs = attn_specs(rows, kv)
    operands = [qkv_t, qkv_t]
    for block in far:
        operands += [block, block]
    table = pl.BlockSpec((HD // 2, rows), lambda g: (0, 0))
    two = pl.BlockSpec((2 * HD, rows), lambda g: (g, 0))
    pair = pl.BlockSpec((2, HD, rows), lambda g: (0, g, 0))
    outs = pl.pallas_call(
        attn_bwd_kernel,
        grid=(kv,),
        in_specs=place_specs
        + [table, table, q_spec]
        + kv_specs
        + [pl.BlockSpec((1, 1, 2 * rows), lambda g: (g, 0, 0)), two, two],
        out_specs=[two, pair, pair, pair, pair],
        out_shape=[jax.ShapeDtypeStruct((2 * kv * HD, rows), BF)]
        + [jax.ShapeDtypeStruct((2, kv * HD, rows), F32)]
        + [jax.ShapeDtypeStruct((2, kv * HD, rows), BF)] * 3,
        compiler_params=pltpu.CompilerParams(vmem_limit_bytes=VMEM_BYTES),
        name="attention_backward",
    )(*places, *tables, qkv_t, *operands, log_total, mixed_t, grad_t)
    return outs


def join_kernel(kv, dq_ref, own_ref, one_ref, two_ref, cos_ref, sin_ref, out_ref, t_ref):
    wide = dq_ref.shape[0]
    half = HD // 2
    cosine, sine = cos_ref[...], sin_ref[...]
    t_ref[:wide] = dq_ref[...].astype(F32)
    dk = own_ref[0] + one_ref[0].astype(F32) + two_ref[0].astype(F32)
    for h in range(kv):
        a = h * HD
        top, low = turned_pair(dk[a : a + half], dk[a + half : a + HD], cosine, -sine)
        t_ref[wide + a : wide + a + half] = top
        t_ref[wide + a + half : wide + a + HD] = low
    t_ref[wide + kv * HD :] = own_ref[1] + one_ref[1].astype(F32) + two_ref[1].astype(F32)
    out_ref[...] = t_ref[...].T.astype(BF)


def join_call(dq, own, one, two, tables, kv):
    rows = dq.shape[1]
    cols = dq.shape[0] + 2 * kv * HD
    return pl.pallas_call(
        functools.partial(join_kernel, kv),
        out_shape=jax.ShapeDtypeStruct((rows, cols), BF),
        scratch_shapes=[pltpu.VMEM((cols, rows), F32)],
        compiler_params=pltpu.CompilerParams(vmem_limit_bytes=VMEM_BYTES),
        name="join_gradients",
    )(dq, own, one, two, *tables)


def halves_of(x, n):
    side = lax.axis_index("dp") % 2
    cols = x.T.reshape(n // 2, 2, x.shape[1] // n, x.shape[0])
    mine = lax.dynamic_index_in_dim(cols, side, 1, keepdims=False)
    other = lax.dynamic_index_in_dim(cols, 1 - side, 1, keepdims=False)
    return mine.reshape(-1, x.shape[0]), other.reshape(-1, x.shape[0])


class Side:
    def __init__(self, mine, theirs):
        self.mine = mine
        self.theirs = theirs


def split_side(x, n):
    mine, other = halves_of(x, n)
    return Side(mine, swap(other, "dp", 1))


def whole_side(x):
    return Side(x, swap(x, "dp", 1))


def weight_grad(left, right):
    total = mm(left.mine, right.mine, 1, 0) + mm(left.theirs, right.theirs, 1, 0)
    return scatter_line(total.astype(BF))


def inverse_rms(x):
    return lax.rsqrt(jnp.mean(x * x, axis=1, keepdims=True) + EPS)


def norm_back(x, inverse, gain, grad, incoming):
    normalized = x * inverse
    scaled = grad * gain
    gain_grad = jnp.sum(grad * normalized, axis=0)
    out = incoming + inverse * (
        scaled - normalized * jnp.mean(scaled * normalized, axis=1, keepdims=True)
    )
    return out, gain_grad


def shards(
    hidden_in,
    doc_lengths,
    norm_attn,
    norm_mlp,
    w_query,
    w_key,
    w_value,
    w_out,
    w_gate,
    w_up,
    w_down,
    cotangent,
):
    rows = hidden_in.shape[0]
    n = lax.axis_size("dp")
    quarter = rows // 4
    pair = rows // 2
    t = lax.axis_index("tensor")
    kv = w_key.shape[2] // HD
    heads = w_query.shape[2] // HD
    seq_count = n // STRETCHES
    shifted = lax.axis_index("dp") + STRETCHES // 2
    stretch = shifted % STRETCHES
    lengths = lax.dynamic_index_in_dim(doc_lengths, shifted // STRETCHES % seq_count, 0, keepdims=False)
    local = jnp.concatenate([(t ^ m) * quarter + jnp.arange(quarter, dtype=jnp.int32) for m in RELATIVE])
    place = stretch * rows + local
    ends = jnp.cumsum(lengths)
    passed = (place[:, None] >= ends[None, :]).astype(jnp.int32)
    start = jnp.sum(passed * lengths[None, :], axis=1)
    frequency = BASE ** (-(jnp.arange(HD // 2, dtype=F32) * 2.0 / HD))
    angles = frequency[:, None] * (place - start).astype(F32)[None, :]
    tables = (jnp.cos(angles), jnp.sin(angles))
    bases = jnp.stack([stretch, stretch ^ 1, stretch - 2, (stretch ^ 1) - 2]) * rows
    places = (bases.astype(jnp.int32), local[:, None], place[None, :], start[None, :])

    w_qkv = jnp.concatenate([w_query, w_key, w_value], axis=2)

    def own_rows(x):
        return lax.dynamic_slice_in_dim(x, t * quarter, quarter, 0)

    flow = own_rows(hidden_in)
    inverse = inverse_rms(flow)
    normed_all = to_relative((hidden_in * inverse_rms(hidden_in) * norm_attn[0]).astype(BF), t)
    records = []
    for l in range(LAYERS):
        qkv_t = qkv_call(normed_all, w_qkv[l], *tables, heads + kv)
        far = keys_onward(qkv_t[heads * HD :])
        mixed_t, log_total = attn_fwd(qkv_t, far, places, kv)
        send = mm(mixed_t[:, pair:], w_out[l], 0, 0).astype(BF)
        keep = mm(mixed_t[:, :pair], w_out[l], 0, 0)
        middle = flow + reduce_rows(keep, send)
        inverse_mlp = inverse_rms(middle)
        normed_mlp = gather_rows((middle * inverse_mlp * norm_mlp[l]).astype(BF))
        gate = mm(normed_mlp, w_gate[l], 1, 0)
        up = mm(normed_mlp, w_up[l], 1, 0)
        activated = (jax.nn.silu(gate) * up).astype(BF)
        send = mm(activated[pair:], w_down[l], 1, 0).astype(BF)
        keep = mm(activated[:pair], w_down[l], 1, 0)
        after = middle + reduce_rows(keep, send)
        records.append(
            (flow, inverse, normed_all, qkv_t, far, mixed_t, log_total, middle, inverse_mlp, normed_mlp, gate, up, activated)
        )
        flow = after
        if l + 1 < LAYERS:
            inverse = inverse_rms(flow)
            normed_all = gather_rows((flow * inverse * norm_attn[l + 1]).astype(BF))
    hidden_out = to_absolute(gather_rows(bf16_of(flow)), t).astype(F32)

    flow = own_rows(cotangent)
    down_in = to_relative(cotangent.astype(BF), t)
    grads = [None] * LAYERS
    gains = [None] * LAYERS
    for l in reversed(range(LAYERS)):
        (before, inverse, normed_all, qkv_t, far, mixed_t, log_total, middle, inverse_mlp, normed_mlp, gate, up, activated) = records[l]
        g_down = weight_grad(split_side(down_in, n), whole_side(activated))
        hidden = mm(down_in, w_down[l], 1, 1)
        sig = jax.nn.sigmoid(gate)
        gate_grad = (hidden * up * sig * (1.0 + gate * (1.0 - sig))).astype(BF)
        up_grad = (hidden * gate * sig).astype(BF)
        send = (mm(gate_grad[pair:], w_gate[l], 1, 1) + mm(up_grad[pair:], w_up[l], 1, 1)).astype(BF)
        keep = mm(gate_grad[:pair], w_gate[l], 1, 1) + mm(up_grad[:pair], w_up[l], 1, 1)
        flow, gain_mlp = norm_back(middle, inverse_mlp, norm_mlp[l], reduce_rows(keep, send), flow)
        normed_side = split_side(normed_mlp, n)
        g_gate = weight_grad(normed_side, whole_side(gate_grad))
        g_up = weight_grad(normed_side, whole_side(up_grad))
        out_in = gather_rows(flow.astype(BF))
        grad_t = mm(w_out[l], out_in, 1, 1).astype(BF)
        dq, own, d_beside, d_behind, d_across = attn_bwd(
            qkv_t, far, places, kv, tables, log_total, mixed_t, grad_t
        )
        g_out = weight_grad(split_side(out_in, n), whole_side(mixed_t.T))
        from_beside, from_behind = keys_back(d_beside, d_behind, d_across)
        d_qkv = join_call(dq, own, from_beside, from_behind, tables, kv)
        send = mm(d_qkv[pair:], w_qkv[l], 1, 1).astype(BF)
        keep = mm(d_qkv[:pair], w_qkv[l], 1, 1)
        flow, gain_attn = norm_back(before, inverse, norm_attn[l], reduce_rows(keep, send), flow)
        g_qkv = weight_grad(split_side(normed_all, n), whole_side(d_qkv))
        if l > 0:
            down_in = gather_rows(flow.astype(BF))
        grads[l] = (g_qkv, g_out, g_gate, g_up, g_down)
        gains[l] = (gain_attn, gain_mlp)
    input_grad = to_absolute(gather_rows(bf16_of(flow)), t).astype(F32)

    early = sum_everywhere(jnp.stack([gains[1][0], gains[1][1], gains[0][1]]))
    late = sum_everywhere(gains[0][0][None])
    width = early.shape[1] // n
    dp = lax.axis_index("dp")
    early = lax.dynamic_slice_in_dim(early, dp * width, width, 1)
    late = lax.dynamic_slice_in_dim(late, dp * width, width, 1)
    norm_attn_grad = jnp.concatenate([late, early[:1]], axis=0)
    norm_mlp_grad = jnp.stack([early[2], early[1]])

    stack = lambda i: jnp.stack([grads[l][i] for l in range(LAYERS)])
    g_qkv = stack(0)
    a, b = heads * HD, (heads + kv) * HD
    turned = lambda i: jnp.stack([grads[l][i].T for l in range(LAYERS)])
    return (
        hidden_out,
        input_grad,
        norm_attn_grad,
        norm_mlp_grad,
        g_qkv[:, :, :a],
        g_qkv[:, :, a:b],
        g_qkv[:, :, b:],
        turned(1),
        stack(2),
        stack(3),
        turned(4),
    )


def solution(mesh):
    placed = (
        P("dp", None),
        P(),
        P(),
        P(),
        P(None, None, "tensor"),
        P(None, None, "tensor"),
        P(None, None, "tensor"),
        P(None, "tensor", None),
        P(None, None, "tensor"),
        P(None, None, "tensor"),
        P(None, "tensor", None),
        P("dp", None),
    )
    return jax.shard_map(
        shards,
        mesh=mesh,
        in_specs=placed,
        out_specs=(
            P("dp", None),
            P("dp", None),
            P(None, "dp"),
            P(None, "dp"),
            P(None, "dp", "tensor"),
            P(None, "dp", "tensor"),
            P(None, "dp", "tensor"),
            P(None, "tensor", "dp"),
            P(None, "dp", "tensor"),
            P(None, "dp", "tensor"),
            P(None, "tensor", "dp"),
        ),
        check_vma=False,
    )
```

```python
import functools

import jax
import jax.numpy as jnp
from jax import lax
from jax.experimental import pallas as pl
from jax.experimental.pallas import tpu as pltpu
from jax.sharding import PartitionSpec as P

HD = 96
LAYERS = 2
STRETCHES = 4
EPS = 1e-05
BASE = 100000.0

BF = jnp.bfloat16
F32 = jnp.float32
NEG = -1e30
VMEM_BYTES = 56 * 2**20


def takes(us):
    return pl.CostEstimate(flops=int(us * 1.1e9), transcendentals=0, bytes_accessed=int(us * 1e6))


def mm(a, b, ca, cb):
    return lax.dot_general(a, b, (((ca,), (cb,)), ((), ())), preferred_element_type=F32)


def after(x, token):
    if token is None:
        return x
    return lax.optimization_barrier((x, token))[0]


def need(*values):
    return lax.optimization_barrier(values)


class Job:
    def __init__(self, make):
        self.make = make
        self.out = None


def window(start, end, jobs):
    if not jobs:
        return end
    leaves, tree = jax.tree.flatten([job.make(start) for job in jobs])
    end, *leaves = need(end, *leaves)
    for job, out in zip(jobs, jax.tree.unflatten(tree, leaves)):
        job.out = out
    return end


def swap(block, axis, mask):
    n = lax.axis_size(axis)
    return lax.ppermute(block, axis, [(i, i ^ mask) for i in range(n)])


def bf16_of(x):
    return lax.reduce_precision(x, 8, 7).astype(BF)


def gather_rows(own, jobs=()):
    beside = window(own, swap(own, "tensor", 2), jobs)
    pair = jnp.concatenate([own, beside], axis=0)
    return jnp.concatenate([pair, swap(pair, "tensor", 1)], axis=0)


def reduce_rows(keep, send, jobs=()):
    quarter = keep.shape[0] // 2
    got = swap(send, "tensor", 1)
    far = (keep[quarter:] + got[quarter:].astype(F32)).astype(BF)
    near = keep[:quarter] + got[:quarter].astype(F32)
    return near + window(far, swap(far, "tensor", 2), jobs).astype(F32)


RELATIVE = (0, 2, 1, 3)


def to_relative(rows, index):
    quarter = rows.shape[0] // 4
    return jnp.concatenate(
        [lax.dynamic_slice_in_dim(rows, (index ^ m) * quarter, quarter, 0) for m in RELATIVE], axis=0
    )


def to_absolute(rows, index):
    quarter = rows.shape[0] // 4
    parts = []
    for j in range(4):
        m = index ^ j
        place = ((m & 1) << 1) | (m >> 1)
        parts.append(lax.dynamic_slice_in_dim(rows, place * quarter, quarter, 0))
    return jnp.concatenate(parts, axis=0)


def in_stretches(pairs_of, n):
    pairs = []
    for i in range(n):
        offset = pairs_of((i + STRETCHES // 2) % STRETCHES)
        if offset is not None:
            pairs.append((i, (i + offset) % n))
    return pairs


def keys_onward(kv):
    n = lax.axis_size("dp")
    across = lax.ppermute(kv, "dp", in_stretches(lambda s: (3, 1, None, None)[s], n))
    behind = lax.ppermute(kv, "dp", in_stretches(lambda s: (2, 2, None, None)[s], n))
    return swap(kv, "dp", 1), behind, across


def keys_back(beside, behind, across):
    n = lax.axis_size("dp")
    across = lax.ppermute(across, "dp", in_stretches(lambda s: (None, None, -1, -3)[s], n))
    behind = lax.ppermute(behind, "dp", in_stretches(lambda s: (None, None, -2, -2)[s], n))
    return swap(beside, "dp", 1), behind, across


def scatter_grad(grad):
    n = lax.axis_size("dp")
    groups = [list(range(side, n, 2)) for side in range(2)]
    out = lax.psum_scatter(
        grad.astype(BF), "dp", scatter_dimension=0, tiled=True, axis_index_groups=groups
    )
    return out.astype(F32)


def sum_everywhere(x):
    x = x + swap(x, "tensor", 1)
    x = x + swap(x, "tensor", 2)
    n = lax.axis_size("dp")
    mask = 1
    while mask < n:
        x = x + swap(x, "dp", mask)
        mask *= 2
    return x


def turned_pair(top, low, cosine, sine):
    return top * cosine - low * sine, low * cosine + top * sine


def qkv_kernel(heads, x_ref, w_ref, cos_ref, sin_ref, out_ref, t_ref):
    t_ref[...] = mm(x_ref[...], w_ref[...], 1, 0).T
    half = HD // 2
    cosine, sine = cos_ref[...], sin_ref[...]
    for h in range(heads):
        a = h * HD
        top, low = turned_pair(t_ref[a : a + half], t_ref[a + half : a + HD], cosine, sine)
        out_ref[a : a + half] = top.astype(BF)
        out_ref[a + half : a + HD] = low.astype(BF)
    rest = heads * HD
    out_ref[rest:] = t_ref[rest:].astype(BF)


def qkv_call(x, w, cosine, sine, heads):
    rows, cols = x.shape[0], w.shape[1]
    return pl.pallas_call(
        functools.partial(qkv_kernel, heads),
        out_shape=jax.ShapeDtypeStruct((cols, rows), BF),
        scratch_shapes=[pltpu.VMEM((cols, rows), F32)],
        compiler_params=pltpu.CompilerParams(vmem_limit_bytes=VMEM_BYTES),
        name="qkv_rotary",
        cost_estimate=takes(4.5),
    )(x, w, cosine, sine)


def both_heads(block):
    return jnp.concatenate([block[:HD], block[HD:]], axis=1)


def flip(block):
    return block.astype(F32).T.astype(BF)


def allowed_of(base, rows_ref, top_ref, start_ref):
    key_place = rows_ref[...] + base
    two = lambda ref: jnp.concatenate([ref[...], ref[...]], axis=1)
    return (key_place >= two(start_ref)) & (key_place <= two(top_ref))


def attn_fwd_kernel(base_ref, rows_ref, top_ref, start_ref, q_ref, *refs):
    keys, values = refs[0:8:2], refs[1:8:2]
    mixed_t_ref, log_ref, s_ref = refs[8:]
    qt = both_heads(q_ref[...])
    top = jnp.full((1, qt.shape[1]), NEG, F32)
    for b in range(4):
        scores = mm(flip(keys[b][...]), qt, 1, 0) * HD ** (-0.5)
        scores = jnp.where(allowed_of(base_ref[b], rows_ref, top_ref, start_ref), scores, NEG)
        s_ref[b] = scores
        top = jnp.maximum(top, jnp.max(scores, axis=0, keepdims=True))
    total = jnp.zeros_like(top)
    acc = jnp.zeros((HD, qt.shape[1]), F32)
    for b in range(4):
        weight = jnp.exp(s_ref[b] - top)
        total = total + jnp.sum(weight, axis=0, keepdims=True)
        acc = acc + mm(values[b][...], weight.astype(BF), 1, 0)
    acc = acc / total
    log_ref[0] = top + jnp.log(total)
    half = qt.shape[1] // 2
    mixed_t_ref[:HD] = acc[:, :half].astype(BF)
    mixed_t_ref[HD:] = acc[:, half:].astype(BF)


def attn_specs(rows, kv):
    q_spec = pl.BlockSpec((2 * HD, rows), lambda g: (g, 0))
    own_k = pl.BlockSpec((HD, rows), lambda g: (2 * kv + g, 0))
    own_v = pl.BlockSpec((HD, rows), lambda g: (3 * kv + g, 0))
    far_k = pl.BlockSpec((HD, rows), lambda g: (g, 0))
    far_v = pl.BlockSpec((HD, rows), lambda g: (kv + g, 0))
    whole = lambda shape: pl.BlockSpec(shape, lambda g: (0,) * len(shape))
    places = [
        pl.BlockSpec(memory_space=pltpu.SMEM),
        whole((rows, 1)),
        whole((1, rows)),
        whole((1, rows)),
    ]
    return places, q_spec, [own_k, own_v] + [far_k, far_v] * 3


def attn_fwd(qkv_t, far, places, kv):
    rows = qkv_t.shape[1]
    place_specs, q_spec, kv_specs = attn_specs(rows, kv)
    operands = [qkv_t, qkv_t]
    for block in far:
        operands += [block, block]
    mixed_t, log_total = pl.pallas_call(
        attn_fwd_kernel,
        grid=(kv,),
        in_specs=place_specs + [q_spec] + kv_specs,
        out_specs=[
            pl.BlockSpec((2 * HD, rows), lambda g: (g, 0)),
            pl.BlockSpec((1, 1, 2 * rows), lambda g: (g, 0, 0)),
        ],
        out_shape=[
            jax.ShapeDtypeStruct((2 * kv * HD, rows), BF),
            jax.ShapeDtypeStruct((kv, 1, 2 * rows), F32),
        ],
        scratch_shapes=[pltpu.VMEM((4, rows, 2 * rows), F32)],
        compiler_params=pltpu.CompilerParams(vmem_limit_bytes=VMEM_BYTES),
        name="attention_forward",
        cost_estimate=takes(11),
    )(*places, qkv_t, *operands)
    return mixed_t, log_total


def attn_bwd_kernel(base_ref, rows_ref, top_ref, start_ref, cos_ref, sin_ref, q_ref, *refs):
    keys, values = refs[0:8:2], refs[1:8:2]
    log_ref, mixed_ref, grad_ref = refs[8:11]
    dq_ref, own_ref, far_refs = refs[11], refs[12], refs[13:]
    qt = both_heads(q_ref[...])
    grad_t = both_heads(grad_ref[...])
    q_rows, grad_rows = flip(qt), flip(grad_t)
    log_total = log_ref[0]
    centre = jnp.sum(
        grad_t.astype(F32) * both_heads(mixed_ref[...]).astype(F32), axis=0, keepdims=True
    )
    dq = jnp.zeros((HD, qt.shape[1]), F32)
    for b in range(4):
        scores = mm(flip(keys[b][...]), qt, 1, 0) * HD ** (-0.5)
        scores = jnp.where(allowed_of(base_ref[b], rows_ref, top_ref, start_ref), scores, NEG)
        probs = jnp.exp(scores - log_total)
        prob_grad = mm(flip(values[b][...]), grad_t, 1, 0)
        score_grad = (probs * (prob_grad - centre) * HD ** (-0.5)).astype(BF)
        dq = dq + mm(keys[b][...], score_grad, 1, 0)
        dv = mm(probs.astype(BF), grad_rows, 1, 0).T
        dk = mm(score_grad, q_rows, 1, 0).T
        out = own_ref if b == 0 else far_refs[b - 1]
        out[0] = dk.astype(out.dtype)
        out[1] = dv.astype(out.dtype)
    half, rows = HD // 2, qt.shape[1] // 2
    cosine, sine = cos_ref[...], sin_ref[...]
    for h in range(2):
        part = dq[:, h * rows : (h + 1) * rows]
        top, low = turned_pair(part[:half], part[half:], cosine, -sine)
        dq_ref[h * HD : h * HD + half] = top.astype(BF)
        dq_ref[h * HD + half : (h + 1) * HD] = low.astype(BF)


def attn_bwd(qkv_t, far, places, kv, tables, log_total, mixed_t, grad_t):
    rows = qkv_t.shape[1]
    place_specs, q_spec, kv_specs = attn_specs(rows, kv)
    operands = [qkv_t, qkv_t]
    for block in far:
        operands += [block, block]
    table = pl.BlockSpec((HD // 2, rows), lambda g: (0, 0))
    two = pl.BlockSpec((2 * HD, rows), lambda g: (g, 0))
    pair = pl.BlockSpec((2, HD, rows), lambda g: (0, g, 0))
    outs = pl.pallas_call(
        attn_bwd_kernel,
        grid=(kv,),
        in_specs=place_specs
        + [table, table, q_spec]
        + kv_specs
        + [pl.BlockSpec((1, 1, 2 * rows), lambda g: (g, 0, 0)), two, two],
        out_specs=[two, pair, pair, pair, pair],
        out_shape=[jax.ShapeDtypeStruct((2 * kv * HD, rows), BF)]
        + [jax.ShapeDtypeStruct((2, kv * HD, rows), F32)]
        + [jax.ShapeDtypeStruct((2, kv * HD, rows), BF)] * 3,
        compiler_params=pltpu.CompilerParams(vmem_limit_bytes=VMEM_BYTES),
        name="attention_backward",
        cost_estimate=takes(16.5),
    )(*places, *tables, qkv_t, *operands, log_total, mixed_t, grad_t)
    return outs


def join_kernel(kv, dq_ref, own_ref, one_ref, two_ref, three_ref, cos_ref, sin_ref, out_ref, t_ref):
    wide = dq_ref.shape[0]
    half = HD // 2
    cosine, sine = cos_ref[...], sin_ref[...]
    t_ref[:wide] = dq_ref[...].astype(F32)
    total = lambda i: own_ref[i] + sum(r[i].astype(F32) for r in (one_ref, two_ref, three_ref))
    dk = total(0)
    for h in range(kv):
        a = h * HD
        top, low = turned_pair(dk[a : a + half], dk[a + half : a + HD], cosine, -sine)
        t_ref[wide + a : wide + a + half] = top
        t_ref[wide + a + half : wide + a + HD] = low
    t_ref[wide + kv * HD :] = total(1)
    out_ref[...] = t_ref[...].T.astype(BF)


def join_call(dq, own, far, tables, kv):
    rows = dq.shape[1]
    cols = dq.shape[0] + 2 * kv * HD
    return pl.pallas_call(
        functools.partial(join_kernel, kv),
        out_shape=jax.ShapeDtypeStruct((rows, cols), BF),
        scratch_shapes=[pltpu.VMEM((cols, rows), F32)],
        compiler_params=pltpu.CompilerParams(vmem_limit_bytes=VMEM_BYTES),
        name="join_gradients",
        cost_estimate=takes(2.8),
    )(dq, own, *far, *tables)


def turned_halves(x, n):
    side = lax.axis_index("dp") % 2
    rows, cols = x.shape
    r, half = cols // n, cols // 2

    def kernel(side_ref, x_ref, mine_ref, other_ref, t_ref):
        t_ref[...] = x_ref[...].astype(F32).T.astype(BF)
        for odd in range(2):

            @pl.when(side_ref[0] == odd)
            def _():
                for b in range(n):
                    to = slice(b // 2 * r, (b // 2 + 1) * r)
                    block = t_ref[b * r : (b + 1) * r]
                    if b % 2 == odd:
                        mine_ref[to] = block
                    else:
                        other_ref[to] = block[:, : rows // 2]

    whole = pl.BlockSpec(memory_space=pltpu.VMEM)
    return pl.pallas_call(
        kernel,
        in_specs=[pl.BlockSpec(memory_space=pltpu.SMEM), whole],
        out_specs=[whole, whole],
        out_shape=[jax.ShapeDtypeStruct((half, rows), BF), jax.ShapeDtypeStruct((half, rows // 2), BF)],
        scratch_shapes=[pltpu.VMEM((cols, rows), BF)],
        compiler_params=pltpu.CompilerParams(vmem_limit_bytes=VMEM_BYTES),
        name="turned_halves",
        cost_estimate=takes(3),
    )(side[None].astype(jnp.int32), x)


class Turned:
    def __init__(self, read, n):
        self.turn = Job(lambda token: turned_halves(after(read(), token), n))
        self.send = Job(lambda token: swap(after(self.turn.out[1], token), "dp", 1))
        self.whole = None

    def parts(self):
        if self.whole is None:
            got = self.send.out
            self.whole = jnp.concatenate([got, swap(got, "tensor", 1)], axis=1)
        return self.turn.out[0], self.whole


class Sent:
    def __init__(self, read, chunks):
        self.read = read
        self.sends = [self.chunk(i, chunks) for i in range(chunks)]

    def chunk(self, i, chunks):
        def make(token):
            x = self.read()
            rows = x.shape[0] // chunks
            return swap(after(x[i * rows : (i + 1) * rows], token), "dp", 1)

        return Job(make)

    def parts(self):
        got = [job.out for job in self.sends]
        return self.read(), got[0] if len(got) == 1 else jnp.concatenate(got, axis=0)


def product(left, right, cb=0):
    def make(token):
        (a, b), (c, d) = left.parts(), right.parts()
        return (mm(a, after(c, token), 1, cb) + mm(b, after(d, token), 1, cb)).astype(BF)

    return Job(make)


def scatter(*products):
    def make(token):
        parts = [p.out for p in products]
        return scatter_grad(parts[0] if len(parts) == 1 else jnp.concatenate(parts, axis=1))

    return Job(make)


def inverse_rms(x):
    return lax.rsqrt(jnp.mean(x * x, axis=1, keepdims=True) + EPS)


def norm_back(x, inverse, gain, grad, incoming):
    normalized = x * inverse
    scaled = grad * gain
    gain_grad = jnp.sum(grad * normalized, axis=0)
    out = incoming + inverse * (
        scaled - normalized * jnp.mean(scaled * normalized, axis=1, keepdims=True)
    )
    return out, gain_grad


def shards(
    hidden_in,
    doc_lengths,
    norm_attn,
    norm_mlp,
    w_query,
    w_key,
    w_value,
    w_out,
    w_gate,
    w_up,
    w_down,
    cotangent,
):
    rows = hidden_in.shape[0]
    n = lax.axis_size("dp")
    quarter = rows // 4
    pair = rows // 2
    t = lax.axis_index("tensor")
    kv = w_key.shape[2] // HD
    heads = w_query.shape[2] // HD
    seq_count = n // STRETCHES
    shifted = lax.axis_index("dp") + STRETCHES // 2
    stretch = shifted % STRETCHES
    lengths = lax.dynamic_index_in_dim(doc_lengths, shifted // STRETCHES % seq_count, 0, keepdims=False)
    local = jnp.concatenate([(t ^ m) * quarter + jnp.arange(quarter, dtype=jnp.int32) for m in RELATIVE])
    place = stretch * rows + local
    ends = jnp.cumsum(lengths)
    passed = (place[:, None] >= ends[None, :]).astype(jnp.int32)
    start = jnp.sum(passed * lengths[None, :], axis=1)
    frequency = BASE ** (-(jnp.arange(HD // 2, dtype=F32) * 2.0 / HD))
    angles = frequency[:, None] * (place - start).astype(F32)[None, :]
    tables = (jnp.cos(angles), jnp.sin(angles))
    bases = jnp.stack([stretch, stretch ^ 1, stretch - 2, (stretch ^ 1) - 2]) * rows
    places = (bases.astype(jnp.int32), local[:, None], place[None, :], start[None, :])

    w_qkv = jnp.concatenate([w_query, w_key, w_value], axis=2)

    def own_rows(x):
        return lax.dynamic_slice_in_dim(x, t * quarter, quarter, 0)

    value = {}

    def later(name, l):
        return lambda: value[name, l]

    layers = range(LAYERS)
    down_left = [Turned(later("down_in", l), n) for l in layers]
    attn_left = [Turned(later("normed", l), n) for l in layers]
    mlp_left = [Turned(later("normed_mlp", l), n) for l in layers]
    out_left = [Turned(later("out_in", l), n) for l in layers]
    act_right = [Sent(later("act", l), 2) for l in layers]
    mixed_right = [Sent(later("mixed", l), 1) for l in layers]
    both_right = [Sent(later("both", l), 4) for l in layers]
    qkv_right = [Sent(later("d_qkv", l), 2) for l in layers]
    g_down = [product(down_left[l], act_right[l]) for l in layers]
    g_both = [product(mlp_left[l], both_right[l]) for l in layers]
    g_out = [product(out_left[l], mixed_right[l], 1) for l in layers]
    g_qkv = [product(attn_left[l], qkv_right[l]) for l in layers]
    s_down = [scatter(g_down[l]) for l in layers]
    s_both = [scatter(g_both[l]) for l in layers]
    s_attn = [scatter(g_out[l], g_qkv[l]) for l in layers]
    plan = {
        ("keys", 0): [down_left[1].turn],
        ("attn", 0): [down_left[1].send],
        ("sum1", 0): [attn_left[0].turn, *mixed_right[0].sends],
        ("all1", 0): [attn_left[0].send],
        ("sum2", 0): [act_right[0].sends[0], mlp_left[0].turn],
        ("all2", 0): [act_right[0].sends[1]],
        ("attn", 1): [mlp_left[0].send],
        ("sum1", 1): [attn_left[1].turn, *mixed_right[1].sends],
        ("all1", 1): [attn_left[1].send],
        ("back_sum1", 1): [both_right[1].sends[0], mlp_left[1].turn],
        ("back_all1", 1): [both_right[1].sends[1]],
        ("back_attn", 1): [both_right[1].sends[2], mlp_left[1].send],
        ("back_keys", 1): [both_right[1].sends[3], out_left[1].turn],
        ("back_join", 1): [act_right[1].sends[0]],
        ("back_sum2", 1): [act_right[1].sends[1], g_both[1]],
        ("back_all2", 1): [out_left[1].send, g_down[1]],
        ("back_gate", 0): [qkv_right[1].sends[0]],
        ("back_mlp", 0): [qkv_right[1].sends[1]],
        ("back_sum1", 0): [both_right[0].sends[0], down_left[0].turn, g_qkv[1], g_out[1], s_both[1]],
        ("back_all1", 0): [both_right[0].sends[1], s_down[1]],
        ("back_attn", 0): both_right[0].sends[2:],
        ("back_keys", 0): [out_left[0].turn, g_both[0], s_attn[1]],
        ("back_join", 0): [down_left[0].send],
        ("back_sum2", 0): [out_left[0].send, g_down[0]],
        ("back_all2", 0): [*qkv_right[0].sends, s_both[0]],
    }
    jobs = lambda name, l: plan.get((name, l), [])

    value["down_in", LAYERS - 1] = to_relative(cotangent.astype(BF), t)
    flow = own_rows(hidden_in)
    inverse = inverse_rms(flow)
    normed_all = to_relative((hidden_in * inverse_rms(hidden_in) * norm_attn[0]).astype(BF), t)
    records = []
    for l in layers:
        value["normed", l] = normed_all
        qkv_t = qkv_call(normed_all, w_qkv[l], *tables, heads + kv)
        far = keys_onward(qkv_t[heads * HD :])
        far = far[:2] + (window(qkv_t, far[2], jobs("keys", l)),)
        mixed_t, log_total = attn_fwd(qkv_t, far, places, kv)
        mixed_t = value["mixed", l] = window(far[2], mixed_t, jobs("attn", l))
        send = mm(mixed_t[:, pair:], w_out[l], 0, 0).astype(BF)
        keep = mm(mixed_t[:, :pair], w_out[l], 0, 0)
        middle = flow + reduce_rows(keep, send, jobs("sum1", l))
        inverse_mlp = inverse_rms(middle)
        normed_mlp = gather_rows((middle * inverse_mlp * norm_mlp[l]).astype(BF), jobs("all1", l))
        value["normed_mlp", l] = normed_mlp
        gate = mm(normed_mlp, w_gate[l], 1, 0)
        up = mm(normed_mlp, w_up[l], 1, 0)
        activated = (jax.nn.silu(gate) * up).astype(BF)
        activated = value["act", l] = window(normed_mlp, activated, jobs("mlp", l))
        send = mm(activated[pair:], w_down[l], 1, 0).astype(BF)
        keep = mm(activated[:pair], w_down[l], 1, 0)
        records.append((flow, inverse, qkv_t, far, log_total, middle, inverse_mlp, gate, up))
        flow = middle + reduce_rows(keep, send, jobs("sum2", l))
        if l + 1 < LAYERS:
            inverse = inverse_rms(flow)
            normed_all = gather_rows((flow * inverse * norm_attn[l + 1]).astype(BF), jobs("all2", l))
    hidden_out = to_absolute(gather_rows(bf16_of(flow)), t).astype(F32)

    flow = own_rows(cotangent)
    gains = [None] * LAYERS
    for l in reversed(layers):
        before, inverse, qkv_t, far, log_total, middle, inverse_mlp, gate, up = records[l]
        down_in = value["down_in", l]
        hidden = mm(down_in, w_down[l], 1, 1)
        sig = jax.nn.sigmoid(gate)
        gate_grad = (hidden * up * sig * (1.0 + gate * (1.0 - sig))).astype(BF)
        up_grad = (hidden * gate * sig).astype(BF)
        both = jnp.concatenate([gate_grad, up_grad], axis=1)
        value["both", l] = window(down_in, both, jobs("back_gate", l))
        send = (mm(gate_grad[pair:], w_gate[l], 1, 1) + mm(up_grad[pair:], w_up[l], 1, 1)).astype(BF)
        keep = mm(gate_grad[:pair], w_gate[l], 1, 1) + mm(up_grad[:pair], w_up[l], 1, 1)
        send = window(both, send, jobs("back_mlp", l))
        total = reduce_rows(keep, send, jobs("back_sum1", l))
        flow, gain_mlp = norm_back(middle, inverse_mlp, norm_mlp[l], total, flow)
        out_in = value["out_in", l] = gather_rows(flow.astype(BF), jobs("back_all1", l))
        grad_t = mm(w_out[l], out_in, 1, 1).astype(BF)
        dq, own, *d_far = attn_bwd(qkv_t, far, places, kv, tables, log_total, value["mixed", l], grad_t)
        dq = window(out_in, dq, jobs("back_attn", l))
        d_far = keys_back(*d_far)
        d_far = d_far[:2] + (window(dq, d_far[2], jobs("back_keys", l)),)
        d_qkv = value["d_qkv", l] = join_call(dq, own, d_far, tables, kv)
        send = mm(d_qkv[pair:], w_qkv[l], 1, 1).astype(BF)
        keep = mm(d_qkv[:pair], w_qkv[l], 1, 1)
        send = window(d_far[2], send, jobs("back_join", l))
        if l + 1 == LAYERS:
            send, hidden_out = need(send, hidden_out)
        total = reduce_rows(keep, send, jobs("back_sum2", l))
        flow, gain_attn = norm_back(before, inverse, norm_attn[l], total, flow)
        gains[l] = (gain_attn, gain_mlp)
        if l > 0:
            value["down_in", l - 1] = gather_rows(flow.astype(BF), jobs("back_all2", l))
    last = gather_rows(bf16_of(flow), jobs("back_all2", 0))
    for job in (s_down[0], g_qkv[0], g_out[0], s_attn[0]):
        job.out = job.make(None)
    input_grad = to_absolute(last, t).astype(F32)

    early = sum_everywhere(jnp.stack([gains[1][0], gains[1][1], gains[0][1]]))
    late = sum_everywhere(gains[0][0][None])
    width = early.shape[1] // n
    dp = lax.axis_index("dp")
    early = lax.dynamic_slice_in_dim(early, dp * width, width, 1)
    late = lax.dynamic_slice_in_dim(late, dp * width, width, 1)
    norm_attn_grad = jnp.concatenate([late, early[:1]], axis=0)
    norm_mlp_grad = jnp.stack([early[2], early[1]])

    def stack(job, start, stop, turn=False):
        parts = [job[l].out[:, start:stop] for l in layers]
        return jnp.stack([p.T if turn else p for p in parts])

    units = w_gate.shape[2]
    a, b, c = heads * HD, 2 * heads * HD, (2 * heads + kv) * HD
    early = (
        hidden_out,
        input_grad,
        norm_attn_grad,
        norm_mlp_grad,
        stack(s_both, 0, units),
        stack(s_both, units, None),
        stack(s_down, 0, None, True),
    )
    *early, s_attn[0].out = need(*early, s_attn[0].out)
    return (
        *early[:4],
        stack(s_attn, a, b),
        stack(s_attn, b, c),
        stack(s_attn, c, None),
        stack(s_attn, 0, a, True),
        *early[4:],
    )


def solution(mesh):
    placed = (
        P("dp", None),
        P(),
        P(),
        P(),
        P(None, None, "tensor"),
        P(None, None, "tensor"),
        P(None, None, "tensor"),
        P(None, "tensor", None),
        P(None, None, "tensor"),
        P(None, None, "tensor"),
        P(None, "tensor", None),
        P("dp", None),
    )
    return jax.shard_map(
        shards,
        mesh=mesh,
        in_specs=placed,
        out_specs=(
            P("dp", None),
            P("dp", None),
            P(None, "dp"),
            P(None, "dp"),
            P(None, "dp", "tensor"),
            P(None, "dp", "tensor"),
            P(None, "dp", "tensor"),
            P(None, "tensor", "dp"),
            P(None, "dp", "tensor"),
            P(None, "dp", "tensor"),
            P(None, "tensor", "dp"),
        ),
        check_vma=False,
    )
```

```python
import functools

import jax
import jax.numpy as jnp
from jax import lax
from jax.experimental import pallas as pl
from jax.experimental.pallas import tpu as pltpu
from jax.sharding import PartitionSpec as P

HD = 96
LAYERS = 2
STRETCHES = 4
EPS = 1e-05
BASE = 100000.0

BF = jnp.bfloat16
F32 = jnp.float32
NEG = -1e30
MIB = 2**20


def takes(us):
    return pl.CostEstimate(flops=int(us * 1.1e9), transcendentals=0, bytes_accessed=int(us * 1e6))


def mm(a, b, ca, cb):
    return lax.dot_general(a, b, (((ca,), (cb,)), ((), ())), preferred_element_type=F32)


def after(x, token):
    if token is None:
        return x
    return lax.optimization_barrier((x, token))[0]


def need(*values):
    return lax.optimization_barrier(values)


class Job:
    def __init__(self, make):
        self.make = make
        self.out = None
        self.raw = None


def window(start, end, jobs):
    if not jobs:
        return end
    for job in jobs:
        job.raw = job.make(start)
    leaves, tree = jax.tree.flatten((end, [job.raw for job in jobs]))
    end, outs = jax.tree.unflatten(tree, need(*leaves))
    for job, out in zip(jobs, outs):
        job.out = out
    return end


def swap(block, axis, mask):
    n = lax.axis_size(axis)
    return lax.ppermute(block, axis, [(i, i ^ mask) for i in range(n)])


def bf16_of(x):
    return lax.reduce_precision(x, 8, 7).astype(BF)


def gather_rows(own, jobs=()):
    beside = window(own, swap(own, "tensor", 2), jobs)
    pair = jnp.concatenate([own, beside], axis=0)
    return jnp.concatenate([pair, swap(pair, "tensor", 1)], axis=0)


def reduce_rows(keep, send, jobs=()):
    quarter = keep.shape[0] // 2
    got = swap(send, "tensor", 1)
    far = (keep[quarter:] + got[quarter:].astype(F32)).astype(BF)
    near = keep[:quarter] + got[:quarter].astype(F32)
    return near + window(far, swap(far, "tensor", 2), jobs).astype(F32)


RELATIVE = (0, 2, 1, 3)


def to_relative(rows, index):
    quarter = rows.shape[0] // 4
    return jnp.concatenate(
        [lax.dynamic_slice_in_dim(rows, (index ^ m) * quarter, quarter, 0) for m in RELATIVE], axis=0
    )


def to_absolute(rows, index):
    quarter = rows.shape[0] // 4
    parts = []
    for j in range(4):
        m = index ^ j
        place = ((m & 1) << 1) | (m >> 1)
        parts.append(lax.dynamic_slice_in_dim(rows, place * quarter, quarter, 0))
    return jnp.concatenate(parts, axis=0)


def in_stretches(pairs_of, n):
    pairs = []
    for i in range(n):
        offset = pairs_of((i + STRETCHES // 2) % STRETCHES)
        if offset is not None:
            pairs.append((i, (i + offset) % n))
    return pairs


def keys_onward(kv):
    n = lax.axis_size("dp")
    across = lax.ppermute(kv, "dp", in_stretches(lambda s: (3, 1, None, None)[s], n))
    behind = lax.ppermute(kv, "dp", in_stretches(lambda s: (2, 2, None, None)[s], n))
    return swap(kv, "dp", 1), behind, across


def keys_back(beside, behind, across):
    n = lax.axis_size("dp")
    late = [i for i in range(n) if (i + STRETCHES // 2) % STRETCHES >= 2]
    across = lax.ppermute(across, "dp", [(i, i ^ 1) for i in late])
    total = (behind.astype(F32) + across.astype(F32)).astype(BF)
    back = in_stretches(lambda s: (None, None, -2, -2)[s], n)
    return swap(beside, "dp", 1), lax.ppermute(total, "dp", back)


def scatter_grad(grad):
    n = lax.axis_size("dp")
    groups = [list(range(side, n, 2)) for side in range(2)]
    out = lax.psum_scatter(
        grad.astype(BF), "dp", scatter_dimension=0, tiled=True, axis_index_groups=groups
    )
    return out.astype(F32)


def sum_everywhere(x):
    x = x + swap(x, "tensor", 1)
    x = x + swap(x, "tensor", 2)
    n = lax.axis_size("dp")
    mask = 1
    while mask < n:
        x = x + swap(x, "dp", mask)
        mask *= 2
    return x


def turned_pair(top, low, cosine, sine):
    return top * cosine - low * sine, low * cosine + top * sine


def layer_block(w, l):
    return pl.BlockSpec((1, *w.shape[1:]), lambda *_: (l, 0, 0))


WHOLE = pl.BlockSpec(memory_space=pltpu.VMEM)


def rotated_rows(out_ref, t, heads, cosine, sine):
    half = HD // 2
    for h in range(heads):
        a = h * HD
        top, low = turned_pair(t[a : a + half], t[a + half : a + HD], cosine, sine)
        out_ref[a : a + half] = top.astype(out_ref.dtype)
        out_ref[a + half : a + HD] = low.astype(out_ref.dtype)


def qkv_kernel(heads, kv, x_ref, wq_ref, wk_ref, wv_ref, cos_ref, sin_ref, q_ref, kv_ref):
    x = x_ref[...]
    cosine, sine = cos_ref[...], sin_ref[...]
    rotated_rows(q_ref, mm(x, wq_ref[0], 1, 0).T, heads, cosine, sine)
    rotated_rows(kv_ref, mm(wk_ref[0], x, 1, 1), kv, cosine, sine)
    kv_ref[kv * HD :] = mm(wv_ref[0], x, 1, 1).astype(BF)


def qkv_call(x, weights, l, tables, heads, kv):
    rows = x.shape[0]
    whole = lambda v: pl.BlockSpec(v.shape, lambda i: (0,) * v.ndim)
    outs = [jax.ShapeDtypeStruct((count * HD, rows), BF) for count in (heads, 2 * kv)]
    return pl.pallas_call(
        functools.partial(qkv_kernel, heads, kv),
        grid=(1,),
        in_specs=[whole(x), *(layer_block(w, l) for w in weights), *(whole(v) for v in tables)],
        out_specs=[whole(v) for v in outs],
        out_shape=outs,
        compiler_params=pltpu.CompilerParams(vmem_limit_bytes=20 * MIB),
        name="qkv_rotary",
        cost_estimate=takes(4.5),
    )(x, *weights, *tables)


def mlp_kernel(x_ref, wg_ref, wu_ref, wd_ref, gate_ref, up_ref, act_ref, keep_ref, send_ref, acc_ref):
    j = pl.program_id(0)
    x = x_ref[...]
    gate, up = mm(x, wg_ref[0], 1, 0), mm(x, wu_ref[0], 1, 0)
    gate_ref[...] = gate
    up_ref[...] = up
    act = (jax.nn.silu(gate) * up).astype(BF)
    act_ref[...] = act
    part = mm(act, wd_ref[0], 1, 0)

    @pl.when(j == 0)
    def _():
        acc_ref[...] = part

    @pl.when(j > 0)
    def _():
        acc_ref[...] += part

    split_sum(j, acc_ref, keep_ref, send_ref)


def split_sum(j, acc_ref, keep_ref, send_ref):
    @pl.when(j == pl.num_programs(0) - 1)
    def _():
        half = keep_ref.shape[0]
        keep_ref[...] = acc_ref[:half]
        send_ref[...] = acc_ref[half:].astype(BF)


UNITS = 512


def mlp_specs(x, l):
    rows, width = x.shape
    whole = lambda shape: pl.BlockSpec(shape, lambda j: (0, 0))
    wide = pl.BlockSpec((1, width, UNITS), lambda j: (l, 0, j))
    tall = pl.BlockSpec((1, UNITS, width), lambda j: (l, j, 0))
    part = pl.BlockSpec((rows, UNITS), lambda j: (0, j))
    sums = [whole((rows // 2, width))] * 2
    sum_shapes = [jax.ShapeDtypeStruct((rows // 2, width), F32), jax.ShapeDtypeStruct((rows // 2, width), BF)]
    return whole((rows, width)), wide, tall, part, sums, sum_shapes


def mlp_call(x, w_gate, w_up, w_down, l):
    whole, wide, tall, part, sums, sum_shapes = mlp_specs(x, l)
    shape = (x.shape[0], w_gate.shape[2])
    return pl.pallas_call(
        mlp_kernel,
        grid=(w_gate.shape[2] // UNITS,),
        in_specs=[whole, wide, wide, tall],
        out_specs=[part, part, part, *sums],
        out_shape=[jax.ShapeDtypeStruct(shape, d) for d in (F32, F32, BF)] + sum_shapes,
        scratch_shapes=[pltpu.VMEM(x.shape, F32)],
        compiler_params=pltpu.CompilerParams(vmem_limit_bytes=30 * MIB),
        name="feed_forward",
        cost_estimate=takes(8),
    )(x, w_gate, w_up, w_down)


def mlp_back_kernel(x_ref, wd_ref, wg_ref, wu_ref, gate_ref, up_ref, gg_ref, ug_ref, keep_ref, send_ref, acc_ref):
    j = pl.program_id(0)
    hidden = mm(x_ref[...], wd_ref[0], 1, 1)
    gate = gate_ref[...]
    sig = jax.nn.sigmoid(gate)
    gg = (hidden * up_ref[...] * sig * (1.0 + gate * (1.0 - sig))).astype(BF)
    ug = (hidden * gate * sig).astype(BF)
    gg_ref[...] = gg
    ug_ref[...] = ug
    part = mm(gg, wg_ref[0], 1, 1) + mm(ug, wu_ref[0], 1, 1)

    @pl.when(j == 0)
    def _():
        acc_ref[...] = part

    @pl.when(j > 0)
    def _():
        acc_ref[...] += part

    split_sum(j, acc_ref, keep_ref, send_ref)


def mlp_back_call(x, w_down, w_gate, w_up, gate, up, l):
    whole, wide, tall, part, sums, sum_shapes = mlp_specs(x, l)
    return pl.pallas_call(
        mlp_back_kernel,
        grid=(w_gate.shape[2] // UNITS,),
        in_specs=[whole, tall, wide, wide, part, part],
        out_specs=[part, part, *sums],
        out_shape=[jax.ShapeDtypeStruct(gate.shape, BF)] * 2 + sum_shapes,
        scratch_shapes=[pltpu.VMEM(x.shape, F32)],
        compiler_params=pltpu.CompilerParams(vmem_limit_bytes=30 * MIB),
        name="feed_forward_back",
        cost_estimate=takes(9),
    )(x, w_down, w_gate, w_up, gate, up)


def both_heads(block):
    return jnp.concatenate([block[:HD], block[HD:]], axis=1)


def flip(block):
    return block.astype(F32).T.astype(BF)


LOG2E = 1.4426950408889634


def fill_bias(base_ref, rows_ref, top_ref, start_ref, bias_ref):
    @pl.when(pl.program_id(0) == 0)
    def _():
        for b in range(4):
            place = rows_ref[...] + base_ref[b]
            allowed = (place >= start_ref[...]) & (place <= top_ref[...])
            bias_ref[b] = jnp.where(allowed, 0.0, NEG)


def scores_of(key, qt, bias):
    return mm(flip(key), qt, 1, 0) * (HD ** (-0.5) * LOG2E) + jnp.concatenate([bias, bias], axis=1)


def attn_fwd_kernel(base_ref, rows_ref, top_ref, start_ref, q_ref, *refs):
    keys, values = refs[0:8:2], refs[1:8:2]
    mixed_t_ref, log_ref, s_ref, bias_ref = refs[8:]
    fill_bias(base_ref, rows_ref, top_ref, start_ref, bias_ref)
    qt = both_heads(q_ref[...])
    top = jnp.full((1, qt.shape[1]), NEG, F32)
    for b in range(4):
        scores = scores_of(keys[b][...], qt, bias_ref[b])
        s_ref[b] = scores
        top = jnp.maximum(top, jnp.max(scores, axis=0, keepdims=True))
    total = jnp.zeros_like(top)
    acc = jnp.zeros((HD, qt.shape[1]), F32)
    for b in range(4):
        weight = jnp.exp2(s_ref[b] - top)
        total = total + jnp.sum(weight, axis=0, keepdims=True)
        acc = acc + mm(values[b][...], weight.astype(BF), 1, 0)
    acc = acc / total
    log_ref[0] = top + jnp.log(total) * LOG2E
    half = qt.shape[1] // 2
    mixed_t_ref[:HD] = acc[:, :half].astype(BF)
    mixed_t_ref[HD:] = acc[:, half:].astype(BF)


def attn_specs(rows, kv):
    q_spec = pl.BlockSpec((2 * HD, rows), lambda g: (g, 0))
    far_k = pl.BlockSpec((HD, rows), lambda g: (g, 0))
    far_v = pl.BlockSpec((HD, rows), lambda g: (kv + g, 0))
    whole = lambda shape: pl.BlockSpec(shape, lambda g: (0,) * len(shape))
    places = [
        pl.BlockSpec(memory_space=pltpu.SMEM),
        whole((rows, 1)),
        whole((1, rows)),
        whole((1, rows)),
    ]
    return places, q_spec, [far_k, far_v] * 4


def attn_fwd(q_t, blocks, places, kv):
    rows = q_t.shape[1]
    place_specs, q_spec, kv_specs = attn_specs(rows, kv)
    operands = [block for block in blocks for _ in range(2)]
    mixed_t, log_total = pl.pallas_call(
        attn_fwd_kernel,
        grid=(kv,),
        in_specs=place_specs + [q_spec] + kv_specs,
        out_specs=[
            pl.BlockSpec((2 * HD, rows), lambda g: (g, 0)),
            pl.BlockSpec((1, 1, 2 * rows), lambda g: (g, 0, 0)),
        ],
        out_shape=[
            jax.ShapeDtypeStruct((2 * kv * HD, rows), BF),
            jax.ShapeDtypeStruct((kv, 1, 2 * rows), F32),
        ],
        scratch_shapes=[pltpu.VMEM((4, rows, 2 * rows), F32), pltpu.VMEM((4, rows, rows), F32)],
        compiler_params=pltpu.CompilerParams(vmem_limit_bytes=24 * MIB),
        name="attention_forward",
        cost_estimate=takes(11),
    )(*places, q_t, *operands)
    return mixed_t, log_total


def attn_bwd_kernel(base_ref, rows_ref, top_ref, start_ref, cos_ref, sin_ref, q_ref, *refs):
    keys, values = refs[0:8:2], refs[1:8:2]
    log_ref, mixed_ref, grad_ref = refs[8:11]
    dq_ref, own_ref, bias_ref = refs[11], refs[12], refs[16]
    far_refs = refs[13:16]
    fill_bias(base_ref, rows_ref, top_ref, start_ref, bias_ref)
    qt = both_heads(q_ref[...])
    grad_t = both_heads(grad_ref[...])
    q_rows, grad_rows = flip(qt), flip(grad_t)
    log_total = log_ref[0]
    centre = jnp.sum(
        grad_t.astype(F32) * both_heads(mixed_ref[...]).astype(F32), axis=0, keepdims=True
    )
    dq = jnp.zeros((HD, qt.shape[1]), F32)
    for b in range(4):
        probs = jnp.exp2(scores_of(keys[b][...], qt, bias_ref[b]) - log_total)
        prob_grad = mm(flip(values[b][...]), grad_t, 1, 0)
        score_grad = (probs * (prob_grad - centre)).astype(BF)
        dq = dq + mm(keys[b][...], score_grad, 1, 0)
        dv = mm(probs.astype(BF), grad_rows, 1, 0).T
        dk = mm(score_grad, q_rows, 1, 0).T * HD ** (-0.5)
        out = own_ref if b == 0 else far_refs[b - 1]
        out[0] = dk.astype(out.dtype)
        out[1] = dv.astype(out.dtype)
    dq = dq * HD ** (-0.5)
    half, rows = HD // 2, qt.shape[1] // 2
    cosine, sine = cos_ref[...], sin_ref[...]
    for h in range(2):
        part = dq[:, h * rows : (h + 1) * rows]
        top, low = turned_pair(part[:half], part[half:], cosine, -sine)
        dq_ref[h * HD : h * HD + half] = top.astype(BF)
        dq_ref[h * HD + half : (h + 1) * HD] = low.astype(BF)


def attn_bwd(q_t, blocks, places, kv, tables, log_total, mixed_t, grad_t):
    rows = q_t.shape[1]
    place_specs, q_spec, kv_specs = attn_specs(rows, kv)
    operands = [block for block in blocks for _ in range(2)]
    table = pl.BlockSpec((HD // 2, rows), lambda g: (0, 0))
    two = pl.BlockSpec((2 * HD, rows), lambda g: (g, 0))
    pair = pl.BlockSpec((2, HD, rows), lambda g: (0, g, 0))
    outs = pl.pallas_call(
        attn_bwd_kernel,
        grid=(kv,),
        in_specs=place_specs
        + [table, table, q_spec]
        + kv_specs
        + [pl.BlockSpec((1, 1, 2 * rows), lambda g: (g, 0, 0)), two, two],
        out_specs=[two, pair, pair, pair, pair],
        out_shape=[jax.ShapeDtypeStruct((2 * kv * HD, rows), BF)]
        + [jax.ShapeDtypeStruct((2, kv * HD, rows), F32)]
        + [jax.ShapeDtypeStruct((2, kv * HD, rows), BF)] * 3,
        scratch_shapes=[pltpu.VMEM((4, rows, rows), F32)],
        compiler_params=pltpu.CompilerParams(vmem_limit_bytes=24 * MIB),
        name="attention_backward",
        cost_estimate=takes(16.5),
    )(*places, *tables, q_t, *operands, log_total, mixed_t, grad_t)
    return outs


def join_kernel(
    kv, dq_ref, own_ref, one_ref, two_ref, cos_ref, sin_ref, wq_ref, wk_ref, wv_ref, *refs
):
    out_ref, keep_ref, send_ref, t_ref = refs
    wide = dq_ref.shape[0]
    cosine, sine = cos_ref[...], sin_ref[...]
    t_ref[:wide] = dq_ref[...].astype(F32)
    total = lambda i: own_ref[i] + sum(r[i].astype(F32) for r in (one_ref, two_ref))
    rotated_rows(t_ref.at[wide : wide + kv * HD], total(0), kv, cosine, -sine)
    t_ref[wide + kv * HD :] = total(1)
    out_ref[...] = t_ref[...].T.astype(BF)
    half = keep_ref.shape[0]
    parts = [
        (out_ref[:, :wide], wq_ref[0], 1),
        (t_ref[wide : wide + kv * HD].T.astype(BF), wk_ref[0], 0),
        (t_ref[wide + kv * HD :].T.astype(BF), wv_ref[0], 0),
    ]
    send_ref[...] = sum(mm(g[half:], w, 1, c) for g, w, c in parts).astype(BF)
    keep_ref[...] = sum(mm(g[:half], w, 1, c) for g, w, c in parts)


def join_call(dq, own, far, tables, weights, l, kv):
    rows = dq.shape[1]
    cols = dq.shape[0] + 2 * kv * HD
    width = weights[0].shape[1]
    whole = lambda v: pl.BlockSpec(v.shape, lambda i: (0,) * len(v.shape))
    outs = [
        jax.ShapeDtypeStruct((rows, cols), BF),
        jax.ShapeDtypeStruct((rows // 2, width), F32),
        jax.ShapeDtypeStruct((rows // 2, width), BF),
    ]
    given = (dq, own, *far, *tables)
    return pl.pallas_call(
        functools.partial(join_kernel, kv),
        grid=(1,),
        in_specs=[whole(v) for v in given] + [layer_block(w, l) for w in weights],
        out_specs=[whole(v) for v in outs],
        out_shape=outs,
        scratch_shapes=[pltpu.VMEM((cols, rows), F32)],
        compiler_params=pltpu.CompilerParams(vmem_limit_bytes=24 * MIB),
        name="join_gradients",
        cost_estimate=takes(5),
    )(*given, *weights)


def turned_halves(x, n):
    side = lax.axis_index("dp") % 2
    rows, cols = x.shape
    r, half = cols // n, cols // 2

    def kernel(side_ref, x_ref, mine_ref, other_ref, t_ref):
        t_ref[...] = x_ref[...].astype(F32).T.astype(BF)
        for odd in range(2):

            @pl.when(side_ref[0] == odd)
            def _():
                for b in range(n):
                    to = slice(b // 2 * r, (b // 2 + 1) * r)
                    block = t_ref[b * r : (b + 1) * r]
                    if b % 2 == odd:
                        mine_ref[to] = block
                    else:
                        other_ref[to] = block[:, : rows // 2]

    whole = pl.BlockSpec(memory_space=pltpu.VMEM)
    return pl.pallas_call(
        kernel,
        in_specs=[pl.BlockSpec(memory_space=pltpu.SMEM), whole],
        out_specs=[whole, whole],
        out_shape=[jax.ShapeDtypeStruct((half, rows), BF), jax.ShapeDtypeStruct((half, rows // 2), BF)],
        scratch_shapes=[pltpu.VMEM((cols, rows), BF)],
        compiler_params=pltpu.CompilerParams(vmem_limit_bytes=12 * MIB),
        name="turned_halves",
        cost_estimate=takes(3),
    )(side[None].astype(jnp.int32), x)


class Turned:
    def __init__(self, read, n):
        self.turn = Job(lambda token: turned_halves(after(read(), token), n))
        self.send = Job(lambda token: swap(after(self.turn.out[1], token), "dp", 1))
        self.whole = None

    def parts(self):
        if self.whole is None:
            got = self.send.out
            self.whole = jnp.concatenate([got, swap(got, "tensor", 1)], axis=1)
        return self.turn.out[0], self.whole


class Sent:
    def __init__(self, read, chunks):
        self.read = read
        self.sends = [self.chunk(i, chunks) for i in range(chunks)]

    def chunk(self, i, chunks):
        def make(token):
            x = self.read()
            rows = x.shape[0] // chunks
            return swap(after(x[i * rows : (i + 1) * rows], token), "dp", 1)

        return Job(make)

    def parts(self):
        got = [job.out for job in self.sends]
        return self.read(), got[0] if len(got) == 1 else jnp.concatenate(got, axis=0)


def product(left, right, cb=0):
    def make(token):
        (a, b), (c, d) = left.parts(), right.parts()
        return (mm(a, after(c, token), 1, cb) + mm(b, after(d, token), 1, cb)).astype(BF)

    return Job(make)


def joined(*products):
    def make(token):
        return jnp.concatenate([p.make(token) if p.raw is None else p.raw for p in products], axis=1)

    return Job(make)


def scatter(before, grad):
    return Job(lambda token: scatter_grad(after(grad.raw, None if before is None else before.raw)))


def inverse_rms(x):
    return lax.rsqrt(jnp.mean(x * x, axis=1, keepdims=True) + EPS)


def norm_back(x, inverse, gain, grad, incoming):
    normalized = x * inverse
    scaled = grad * gain
    gain_grad = jnp.sum(grad * normalized, axis=0)
    out = incoming + inverse * (
        scaled - normalized * jnp.mean(scaled * normalized, axis=1, keepdims=True)
    )
    return out, gain_grad


def shards(
    hidden_in,
    doc_lengths,
    norm_attn,
    norm_mlp,
    w_query,
    w_key,
    w_value,
    w_out,
    w_gate,
    w_up,
    w_down,
    cotangent,
):
    rows = hidden_in.shape[0]
    n = lax.axis_size("dp")
    quarter = rows // 4
    pair = rows // 2
    t = lax.axis_index("tensor")
    kv = w_key.shape[2] // HD
    heads = w_query.shape[2] // HD
    seq_count = n // STRETCHES
    shifted = lax.axis_index("dp") + STRETCHES // 2
    stretch = shifted % STRETCHES
    lengths = lax.dynamic_index_in_dim(doc_lengths, shifted // STRETCHES % seq_count, 0, keepdims=False)
    local = jnp.concatenate([(t ^ m) * quarter + jnp.arange(quarter, dtype=jnp.int32) for m in RELATIVE])
    place = stretch * rows + local
    ends = jnp.cumsum(lengths)
    passed = (place[:, None] >= ends[None, :]).astype(jnp.int32)
    start = jnp.sum(passed * lengths[None, :], axis=1)
    frequency = BASE ** (-(jnp.arange(HD // 2, dtype=F32) * 2.0 / HD))
    angles = frequency[:, None] * (place - start).astype(F32)[None, :]
    tables = (jnp.cos(angles), jnp.sin(angles))
    bases = jnp.stack([stretch, stretch ^ 1, stretch - 2, (stretch ^ 1) - 2]) * rows
    places = (bases.astype(jnp.int32), local[:, None], place[None, :], start[None, :])

    w_qkv = (w_query, jnp.swapaxes(w_key, 1, 2), jnp.swapaxes(w_value, 1, 2))

    def own_rows(x):
        return lax.dynamic_slice_in_dim(x, t * quarter, quarter, 0)

    value = {}

    def later(name, l):
        return lambda: value[name, l]

    layers = range(LAYERS)
    down_left = [Turned(later("down_in", l), n) for l in layers]
    attn_left = [Turned(later("normed", l), n) for l in layers]
    mlp_left = [Turned(later("normed_mlp", l), n) for l in layers]
    out_left = [Turned(later("out_in", l), n) for l in layers]
    act_right = [Sent(later("act", l), 2) for l in layers]
    mixed_right = [Sent(later("mixed", l), 1) for l in layers]
    gate_right = [Sent(later("gate", l), 2) for l in layers]
    up_right = [Sent(later("up", l), 2) for l in layers]
    qkv_right = [Sent(later("d_qkv", l), 2) for l in layers]
    g_down = [product(down_left[l], act_right[l]) for l in layers]
    g_gate = [product(mlp_left[l], gate_right[l]) for l in layers]
    g_up = [product(mlp_left[l], up_right[l]) for l in layers]
    g_out = [product(out_left[l], mixed_right[l], 1) for l in layers]
    g_qkv = [product(attn_left[l], qkv_right[l]) for l in layers]
    g_both = joined(g_gate[0], g_up[0])
    g_more = joined(g_up[1], g_down[1])
    g_attn = [joined(g_out[l], g_qkv[l]) for l in layers]
    s_gate = scatter(None, g_gate[1])
    s_more = scatter(s_gate, g_more)
    s_attn = [None, scatter(s_more, g_attn[1])]
    s_both = scatter(s_attn[1], g_both)
    s_down = scatter(s_both, g_down[0])
    s_attn[0] = scatter(s_down, g_attn[0])
    plan = {
        ("keys", 0): [down_left[1].turn],
        ("attn", 0): [down_left[1].send],
        ("sum1", 0): [attn_left[0].turn, *mixed_right[0].sends],
        ("all1", 0): [attn_left[0].send],
        ("sum2", 0): [act_right[0].sends[0], mlp_left[0].turn],
        ("all2", 0): [act_right[0].sends[1]],
        ("attn", 1): [mlp_left[0].send],
        ("sum1", 1): [attn_left[1].turn, *mixed_right[1].sends],
        ("all1", 1): [attn_left[1].send],
        ("back_sum1", 1): [gate_right[1].sends[0], mlp_left[1].turn],
        ("back_all1", 1): [gate_right[1].sends[1]],
        ("back_attn", 1): [mlp_left[1].send, up_right[1].sends[0]],
        ("back_keys", 1): [up_right[1].sends[1], out_left[1].turn, g_gate[1]],
        ("back_join", 1): [act_right[1].sends[0]],
        ("back_sum2", 1): [act_right[1].sends[1], g_up[1]],
        ("back_all2", 1): [out_left[1].send, g_more],
        ("back_mlp", 0): [qkv_right[1].sends[0], s_gate],
        ("back_sum1", 0): [qkv_right[1].sends[1], gate_right[0].sends[0], down_left[0].turn],
        ("back_all1", 0): [gate_right[0].sends[1], g_attn[1], s_more],
        ("back_attn", 0): [*up_right[0].sends],
        ("back_keys", 0): [g_both, out_left[0].turn, s_attn[1]],
        ("back_join", 0): [down_left[0].send],
        ("back_sum2", 0): [out_left[0].send, qkv_right[0].sends[0], g_down[0], s_both],
        ("back_all2", 0): [qkv_right[0].sends[1]],
    }
    jobs = lambda name, l: plan.get((name, l), [])

    value["down_in", LAYERS - 1] = to_relative(cotangent.astype(BF), t)
    flow = own_rows(hidden_in)
    inverse = inverse_rms(flow)
    normed_all = to_relative((hidden_in * inverse_rms(hidden_in) * norm_attn[0]).astype(BF), t)
    records = []
    for l in layers:
        value["normed", l] = normed_all
        q_t, kv_t = qkv_call(normed_all, w_qkv, l, tables, heads, kv)
        beside, behind, across = keys_onward(kv_t)
        across = window(kv_t, across, jobs("keys", l))
        blocks = (kv_t, beside, behind, across)
        mixed_t, log_total = attn_fwd(q_t, blocks, places, kv)
        mixed_t = value["mixed", l] = window(across, mixed_t, jobs("attn", l))
        send = mm(mixed_t[:, pair:], w_out[l], 0, 0).astype(BF)
        keep = mm(mixed_t[:, :pair], w_out[l], 0, 0)
        middle = flow + reduce_rows(keep, send, jobs("sum1", l))
        inverse_mlp = inverse_rms(middle)
        normed_mlp = gather_rows((middle * inverse_mlp * norm_mlp[l]).astype(BF), jobs("all1", l))
        value["normed_mlp", l] = normed_mlp
        gate, up, value["act", l], keep, send = mlp_call(normed_mlp, w_gate, w_up, w_down, l)
        send = window(normed_mlp, send, jobs("mlp", l))
        records.append((flow, inverse, q_t, blocks, log_total, middle, inverse_mlp, gate, up))
        if l + 1 < LAYERS:
            flow = middle + reduce_rows(keep, send, jobs("sum2", l))
            inverse = inverse_rms(flow)
            normed_all = gather_rows((flow * inverse * norm_attn[l + 1]).astype(BF), jobs("all2", l))

    def output_of(token):
        out = bf16_of(middle_last + reduce_rows(keep_last, after(send_last, token)))
        return to_absolute(gather_rows(out), t).astype(F32)

    middle_last, keep_last, send_last = middle, keep, send

    flow = own_rows(cotangent)
    gains = [None] * LAYERS
    for l in reversed(layers):
        before, inverse, q_t, blocks, log_total, middle, inverse_mlp, gate, up = records[l]
        down_in = value["down_in", l]
        gate_grad, up_grad, keep, send = mlp_back_call(down_in, w_down, w_gate, w_up, gate, up, l)
        value["gate", l], value["up", l] = gate_grad, up_grad
        send = window(down_in, send, jobs("back_mlp", l))
        total = reduce_rows(keep, send, jobs("back_sum1", l))
        flow, gain_mlp = norm_back(middle, inverse_mlp, norm_mlp[l], total, flow)
        out_in = value["out_in", l] = gather_rows(flow.astype(BF), jobs("back_all1", l))
        grad_t = mm(w_out[l], out_in, 1, 1).astype(BF)
        dq, own, *d_far = attn_bwd(q_t, blocks, places, kv, tables, log_total, value["mixed", l], grad_t)
        dq, d_far = window(out_in, (dq, d_far), jobs("back_attn", l))
        d_far = keys_back(*d_far)
        d_far = (d_far[0], window(dq, d_far[1], jobs("back_keys", l)))
        d_qkv, keep, send = join_call(dq, own, d_far, tables, w_qkv, l, kv)
        value["d_qkv", l] = d_qkv
        send = window(d_far[1], send, jobs("back_join", l))
        if l + 1 == LAYERS:
            send, hidden_out = need(send, output_of(out_in))
        total = reduce_rows(keep, send, jobs("back_sum2", l))
        flow, gain_attn = norm_back(before, inverse, norm_attn[l], total, flow)
        gains[l] = (gain_attn, gain_mlp)
        if l > 0:
            value["down_in", l - 1] = gather_rows(flow.astype(BF), jobs("back_all2", l))
    final = gather_rows(bf16_of(flow), jobs("back_all2", 0))
    for job in (s_down, g_attn[0], s_attn[0]):
        job.out = job.raw = job.make(None)
    input_grad = to_absolute(final, t).astype(F32)

    gain_grads = jnp.stack([gains[0][0], gains[1][0], gains[0][1], gains[1][1]])
    gain_grads = sum_everywhere(after(gain_grads, g_attn[0].raw))
    width = gain_grads.shape[1] // n
    gain_grads = lax.dynamic_slice_in_dim(gain_grads, lax.axis_index("dp") * width, width, 1)
    norm_attn_grad, norm_mlp_grad = gain_grads[:LAYERS], gain_grads[LAYERS:]

    def stack(parts, turn=False):
        return jnp.stack([p.T if turn else p for p in parts])

    units = w_gate.shape[2]
    a, b, c = heads * HD, 2 * heads * HD, (2 * heads + kv) * HD
    early = (
        hidden_out,
        input_grad,
        norm_attn_grad,
        norm_mlp_grad,
        stack([s_both.out[:, :units], s_gate.out]),
        stack([s_both.out[:, units:], s_more.out[:, :units]]),
        stack([s_down.out, s_more.out[:, units:]], True),
    )
    *early, s_attn[0].out = need(*early, s_attn[0].out)
    attn = lambda start, stop: [job.out[:, start:stop] for job in s_attn]
    return (
        *early[:4],
        stack(attn(a, b)),
        stack(attn(b, c)),
        stack(attn(c, None)),
        stack(attn(0, a), True),
        *early[4:],
    )


def solution(mesh):
    placed = (
        P("dp", None),
        P(),
        P(),
        P(),
        P(None, None, "tensor"),
        P(None, None, "tensor"),
        P(None, None, "tensor"),
        P(None, "tensor", None),
        P(None, None, "tensor"),
        P(None, None, "tensor"),
        P(None, "tensor", None),
        P("dp", None),
    )
    return jax.shard_map(
        shards,
        mesh=mesh,
        in_specs=placed,
        out_specs=(
            P("dp", None),
            P("dp", None),
            P(None, "dp"),
            P(None, "dp"),
            P(None, "dp", "tensor"),
            P(None, "dp", "tensor"),
            P(None, "dp", "tensor"),
            P(None, "tensor", "dp"),
            P(None, "dp", "tensor"),
            P(None, "dp", "tensor"),
            P(None, "tensor", "dp"),
        ),
        check_vma=False,
    )
```

```python
import functools

import jax
import jax.numpy as jnp
from jax import lax
from jax.experimental import pallas as pl
from jax.experimental.pallas import tpu as pltpu
from jax.sharding import PartitionSpec as P

HD = 96
LAYERS = 2
STRETCHES = 4
EPS = 1e-05
BASE = 100000.0

BF = jnp.bfloat16
F32 = jnp.float32
NEG = -1e30
MIB = 2**20


def takes(us):
    return pl.CostEstimate(flops=int(us * 1.1e9), transcendentals=0, bytes_accessed=int(us * 1e6))


def mm(a, b, ca, cb):
    return lax.dot_general(a, b, (((ca,), (cb,)), ((), ())), preferred_element_type=F32)


def after(x, token):
    if token is None:
        return x
    return lax.optimization_barrier((x, token))[0]


def need(*values):
    return lax.optimization_barrier(values)


class Job:
    def __init__(self, make):
        self.make = make
        self.out = None
        self.raw = None


def window(start, end, jobs):
    if not jobs:
        return end
    for job in jobs:
        job.raw = job.make(start)
    leaves, tree = jax.tree.flatten((end, [job.raw for job in jobs]))
    end, outs = jax.tree.unflatten(tree, need(*leaves))
    for job, out in zip(jobs, outs):
        job.out = out
    return end


def swap(block, axis, mask):
    n = lax.axis_size(axis)
    return lax.ppermute(block, axis, [(i, i ^ mask) for i in range(n)])


def bf16_of(x):
    return lax.reduce_precision(x, 8, 7).astype(BF)


def gather_rows(own, jobs=()):
    beside = window(own, swap(own, "tensor", 2), jobs)
    pair = jnp.concatenate([own, beside], axis=0)
    return jnp.concatenate([pair, swap(pair, "tensor", 1)], axis=0)


def reduce_rows(keep, send, jobs=()):
    quarter = keep.shape[0] // 2
    got = swap(send, "tensor", 1)
    far = (keep[quarter:] + got[quarter:].astype(F32)).astype(BF)
    near = keep[:quarter] + got[:quarter].astype(F32)
    return near + window(far, swap(far, "tensor", 2), jobs).astype(F32)


RELATIVE = (0, 2, 1, 3)


def to_relative(rows, index):
    quarter = rows.shape[0] // 4
    return jnp.concatenate(
        [lax.dynamic_slice_in_dim(rows, (index ^ m) * quarter, quarter, 0) for m in RELATIVE], axis=0
    )


def to_absolute(rows, index):
    quarter = rows.shape[0] // 4
    parts = []
    for j in range(4):
        m = index ^ j
        place = ((m & 1) << 1) | (m >> 1)
        parts.append(lax.dynamic_slice_in_dim(rows, place * quarter, quarter, 0))
    return jnp.concatenate(parts, axis=0)


def in_stretches(pairs_of, n):
    pairs = []
    for i in range(n):
        offset = pairs_of((i + STRETCHES // 2) % STRETCHES)
        if offset is not None:
            pairs.append((i, (i + offset) % n))
    return pairs


def keys_onward(kv):
    n = lax.axis_size("dp")
    across = lax.ppermute(kv, "dp", in_stretches(lambda s: (3, 1, None, None)[s], n))
    behind = lax.ppermute(kv, "dp", in_stretches(lambda s: (2, 2, None, None)[s], n))
    return swap(kv, "dp", 1), behind, across


def keys_back(beside, behind, across, jobs):
    n = lax.axis_size("dp")
    late = [i for i in range(n) if (i + STRETCHES // 2) % STRETCHES >= 2]
    across = window(across, lax.ppermute(across, "dp", [(i, i ^ 1) for i in late]), jobs)
    total = (behind.astype(F32) + across.astype(F32)).astype(BF)
    back = in_stretches(lambda s: (None, None, -2, -2)[s], n)
    return total, swap(beside, "dp", 1), lax.ppermute(total, "dp", back)


def scatter_grad(grad):
    n = lax.axis_size("dp")
    groups = [list(range(side, n, 2)) for side in range(2)]
    out = lax.psum_scatter(
        grad.astype(BF), "dp", scatter_dimension=0, tiled=True, axis_index_groups=groups
    )
    return out.astype(F32)


def sum_everywhere(x):
    x = x + swap(x, "tensor", 1)
    x = x + swap(x, "tensor", 2)
    n = lax.axis_size("dp")
    mask = 1
    while mask < n:
        x = x + swap(x, "dp", mask)
        mask *= 2
    return x


def turned_pair(top, low, cosine, sine):
    return top * cosine - low * sine, low * cosine + top * sine


def layer_block(w, l):
    return pl.BlockSpec((1, *w.shape[1:]), lambda *_: (l, 0, 0))


WHOLE = pl.BlockSpec(memory_space=pltpu.VMEM)


def rotated_rows(out_ref, t, heads, cosine, sine):
    half = HD // 2
    for h in range(heads):
        a = h * HD
        top, low = turned_pair(t[a : a + half], t[a + half : a + HD], cosine, sine)
        out_ref[a : a + half] = top.astype(out_ref.dtype)
        out_ref[a + half : a + HD] = low.astype(out_ref.dtype)


def qkv_kernel(heads, kv, x_ref, wq_ref, wk_ref, wv_ref, cos_ref, sin_ref, q_ref, kv_ref):
    x = x_ref[...]
    cosine, sine = cos_ref[...], sin_ref[...]
    rotated_rows(q_ref, mm(x, wq_ref[0], 1, 0).T, heads, cosine, sine)
    rotated_rows(kv_ref, mm(wk_ref[0], x, 1, 1), kv, cosine, sine)
    kv_ref[kv * HD :] = mm(wv_ref[0], x, 1, 1).astype(BF)


def qkv_call(x, weights, l, tables, heads, kv):
    rows = x.shape[0]
    whole = lambda v: pl.BlockSpec(v.shape, lambda i: (0,) * v.ndim)
    outs = [jax.ShapeDtypeStruct((count * HD, rows), BF) for count in (heads, 2 * kv)]
    return pl.pallas_call(
        functools.partial(qkv_kernel, heads, kv),
        grid=(1,),
        in_specs=[whole(x), *(layer_block(w, l) for w in weights), *(whole(v) for v in tables)],
        out_specs=[whole(v) for v in outs],
        out_shape=outs,
        compiler_params=pltpu.CompilerParams(vmem_limit_bytes=20 * MIB),
        name="qkv_rotary",
        cost_estimate=takes(4.5),
    )(x, *weights, *tables)


def mlp_kernel(x_ref, wg_ref, wu_ref, wd_ref, gate_ref, up_ref, act_ref, keep_ref, send_ref, acc_ref):
    j = pl.program_id(0)
    x = x_ref[...]
    gate, up = mm(x, wg_ref[0], 1, 0), mm(x, wu_ref[0], 1, 0)
    gate_ref[...] = gate
    up_ref[...] = up
    act = (jax.nn.silu(gate) * up).astype(BF)
    act_ref[...] = act
    part = mm(act, wd_ref[0], 1, 0)

    @pl.when(j == 0)
    def _():
        acc_ref[...] = part

    @pl.when(j > 0)
    def _():
        acc_ref[...] += part

    split_sum(j, acc_ref, keep_ref, send_ref)


def split_sum(j, acc_ref, keep_ref, send_ref):
    @pl.when(j == pl.num_programs(0) - 1)
    def _():
        half = keep_ref.shape[0]
        keep_ref[...] = acc_ref[:half]
        send_ref[...] = acc_ref[half:].astype(BF)


UNITS = 512


def mlp_specs(x, l):
    rows, width = x.shape
    whole = lambda shape: pl.BlockSpec(shape, lambda j: (0, 0))
    wide = pl.BlockSpec((1, width, UNITS), lambda j: (l, 0, j))
    tall = pl.BlockSpec((1, UNITS, width), lambda j: (l, j, 0))
    part = pl.BlockSpec((rows, UNITS), lambda j: (0, j))
    sums = [whole((rows // 2, width))] * 2
    sum_shapes = [jax.ShapeDtypeStruct((rows // 2, width), F32), jax.ShapeDtypeStruct((rows // 2, width), BF)]
    return whole((rows, width)), wide, tall, part, sums, sum_shapes


def mlp_call(x, w_gate, w_up, w_down, l):
    whole, wide, tall, part, sums, sum_shapes = mlp_specs(x, l)
    shape = (x.shape[0], w_gate.shape[2])
    return pl.pallas_call(
        mlp_kernel,
        grid=(w_gate.shape[2] // UNITS,),
        in_specs=[whole, wide, wide, tall],
        out_specs=[part, part, part, *sums],
        out_shape=[jax.ShapeDtypeStruct(shape, d) for d in (F32, F32, BF)] + sum_shapes,
        scratch_shapes=[pltpu.VMEM(x.shape, F32)],
        compiler_params=pltpu.CompilerParams(vmem_limit_bytes=30 * MIB),
        name="feed_forward",
        cost_estimate=takes(8),
    )(x, w_gate, w_up, w_down)


def mlp_back_kernel(x_ref, wd_ref, wg_ref, wu_ref, gate_ref, up_ref, gg_ref, ug_ref, keep_ref, send_ref, acc_ref):
    j = pl.program_id(0)
    hidden = mm(x_ref[...], wd_ref[0], 1, 1)
    gate = gate_ref[...]
    sig = jax.nn.sigmoid(gate)
    gg = (hidden * up_ref[...] * sig * (1.0 + gate * (1.0 - sig))).astype(BF)
    ug = (hidden * gate * sig).astype(BF)
    gg_ref[...] = gg
    ug_ref[...] = ug
    part = mm(gg, wg_ref[0], 1, 1) + mm(ug, wu_ref[0], 1, 1)

    @pl.when(j == 0)
    def _():
        acc_ref[...] = part

    @pl.when(j > 0)
    def _():
        acc_ref[...] += part

    split_sum(j, acc_ref, keep_ref, send_ref)


def mlp_back_call(x, w_down, w_gate, w_up, gate, up, l):
    whole, wide, tall, part, sums, sum_shapes = mlp_specs(x, l)
    return pl.pallas_call(
        mlp_back_kernel,
        grid=(w_gate.shape[2] // UNITS,),
        in_specs=[whole, tall, wide, wide, part, part],
        out_specs=[part, part, *sums],
        out_shape=[jax.ShapeDtypeStruct(gate.shape, BF)] * 2 + sum_shapes,
        scratch_shapes=[pltpu.VMEM(x.shape, F32)],
        compiler_params=pltpu.CompilerParams(vmem_limit_bytes=30 * MIB),
        name="feed_forward_back",
        cost_estimate=takes(9),
    )(x, w_down, w_gate, w_up, gate, up)


def both_heads(block):
    return jnp.concatenate([block[:HD], block[HD:]], axis=1)


def flip(block):
    return block.astype(F32).T.astype(BF)


LOG2E = 1.4426950408889634


def fill_bias(base_ref, rows_ref, top_ref, start_ref, bias_ref):
    @pl.when(pl.program_id(0) == 0)
    def _():
        for b in range(4):
            place = rows_ref[...] + base_ref[b]
            allowed = (place >= start_ref[...]) & (place <= top_ref[...])
            bias_ref[b] = jnp.where(allowed, 0.0, NEG)


def scores_of(key, qt, bias):
    return mm(flip(key), qt, 1, 0) * (HD ** (-0.5) * LOG2E) + jnp.concatenate([bias, bias], axis=1)


def attn_fwd_kernel(base_ref, rows_ref, top_ref, start_ref, q_ref, *refs):
    keys, values = refs[0:8:2], refs[1:8:2]
    mixed_t_ref, log_ref, s_ref, bias_ref = refs[8:]
    fill_bias(base_ref, rows_ref, top_ref, start_ref, bias_ref)
    qt = both_heads(q_ref[...])
    top = jnp.full((1, qt.shape[1]), NEG, F32)
    for b in range(4):
        scores = scores_of(keys[b][...], qt, bias_ref[b])
        s_ref[b] = scores
        top = jnp.maximum(top, jnp.max(scores, axis=0, keepdims=True))
    total = jnp.zeros_like(top)
    acc = jnp.zeros((HD, qt.shape[1]), F32)
    for b in range(4):
        weight = jnp.exp2(s_ref[b] - top)
        total = total + jnp.sum(weight, axis=0, keepdims=True)
        acc = acc + mm(values[b][...], weight.astype(BF), 1, 0)
    acc = acc / total
    log_ref[0] = top + jnp.log(total) * LOG2E
    half = qt.shape[1] // 2
    mixed_t_ref[:HD] = acc[:, :half].astype(BF)
    mixed_t_ref[HD:] = acc[:, half:].astype(BF)


def attn_specs(rows, kv):
    q_spec = pl.BlockSpec((2 * HD, rows), lambda g: (g, 0))
    far_k = pl.BlockSpec((HD, rows), lambda g: (g, 0))
    far_v = pl.BlockSpec((HD, rows), lambda g: (kv + g, 0))
    whole = lambda shape: pl.BlockSpec(shape, lambda g: (0,) * len(shape))
    places = [
        pl.BlockSpec(memory_space=pltpu.SMEM),
        whole((rows, 1)),
        whole((1, rows)),
        whole((1, rows)),
    ]
    return places, q_spec, [far_k, far_v] * 4


def attn_fwd(q_t, blocks, places, kv):
    rows = q_t.shape[1]
    place_specs, q_spec, kv_specs = attn_specs(rows, kv)
    operands = [block for block in blocks for _ in range(2)]
    mixed_t, log_total = pl.pallas_call(
        attn_fwd_kernel,
        grid=(kv,),
        in_specs=place_specs + [q_spec] + kv_specs,
        out_specs=[
            pl.BlockSpec((2 * HD, rows), lambda g: (g, 0)),
            pl.BlockSpec((1, 1, 2 * rows), lambda g: (g, 0, 0)),
        ],
        out_shape=[
            jax.ShapeDtypeStruct((2 * kv * HD, rows), BF),
            jax.ShapeDtypeStruct((kv, 1, 2 * rows), F32),
        ],
        scratch_shapes=[pltpu.VMEM((4, rows, 2 * rows), F32), pltpu.VMEM((4, rows, rows), F32)],
        compiler_params=pltpu.CompilerParams(vmem_limit_bytes=24 * MIB),
        name="attention_forward",
        cost_estimate=takes(11),
    )(*places, q_t, *operands)
    return mixed_t, log_total


def attn_bwd_kernel(base_ref, rows_ref, top_ref, start_ref, cos_ref, sin_ref, q_ref, *refs):
    keys, values = refs[0:8:2], refs[1:8:2]
    log_ref, mixed_ref, grad_ref = refs[8:11]
    dq_ref, own_ref, bias_ref = refs[11], refs[12], refs[16]
    far_refs = refs[13:16]
    fill_bias(base_ref, rows_ref, top_ref, start_ref, bias_ref)
    qt = both_heads(q_ref[...])
    grad_t = both_heads(grad_ref[...])
    q_rows, grad_rows = flip(qt), flip(grad_t)
    log_total = log_ref[0]
    centre = jnp.sum(
        grad_t.astype(F32) * both_heads(mixed_ref[...]).astype(F32), axis=0, keepdims=True
    )
    dq = jnp.zeros((HD, qt.shape[1]), F32)
    for b in range(4):
        probs = jnp.exp2(scores_of(keys[b][...], qt, bias_ref[b]) - log_total)
        prob_grad = mm(flip(values[b][...]), grad_t, 1, 0)
        score_grad = (probs * (prob_grad - centre)).astype(BF)
        dq = dq + mm(keys[b][...], score_grad, 1, 0)
        dv = mm(probs.astype(BF), grad_rows, 1, 0).T
        dk = mm(score_grad, q_rows, 1, 0).T * HD ** (-0.5)
        out = own_ref if b == 0 else far_refs[b - 1]
        out[0] = dk.astype(out.dtype)
        out[1] = dv.astype(out.dtype)
    dq = dq * HD ** (-0.5)
    half, rows = HD // 2, qt.shape[1] // 2
    cosine, sine = cos_ref[...], sin_ref[...]
    for h in range(2):
        part = dq[:, h * rows : (h + 1) * rows]
        top, low = turned_pair(part[:half], part[half:], cosine, -sine)
        dq_ref[h * HD : h * HD + half] = top.astype(BF)
        dq_ref[h * HD + half : (h + 1) * HD] = low.astype(BF)


def attn_bwd(q_t, blocks, places, kv, tables, log_total, mixed_t, grad_t):
    rows = q_t.shape[1]
    place_specs, q_spec, kv_specs = attn_specs(rows, kv)
    operands = [block for block in blocks for _ in range(2)]
    table = pl.BlockSpec((HD // 2, rows), lambda g: (0, 0))
    two = pl.BlockSpec((2 * HD, rows), lambda g: (g, 0))
    pair = pl.BlockSpec((2, HD, rows), lambda g: (0, g, 0))
    outs = pl.pallas_call(
        attn_bwd_kernel,
        grid=(kv,),
        in_specs=place_specs
        + [table, table, q_spec]
        + kv_specs
        + [pl.BlockSpec((1, 1, 2 * rows), lambda g: (g, 0, 0)), two, two],
        out_specs=[two, pair, pair, pair, pair],
        out_shape=[jax.ShapeDtypeStruct((2 * kv * HD, rows), BF)]
        + [jax.ShapeDtypeStruct((2, kv * HD, rows), F32)]
        + [jax.ShapeDtypeStruct((2, kv * HD, rows), BF)] * 3,
        scratch_shapes=[pltpu.VMEM((4, rows, rows), F32)],
        compiler_params=pltpu.CompilerParams(vmem_limit_bytes=24 * MIB),
        name="attention_backward",
        cost_estimate=takes(16.5),
    )(*places, *tables, q_t, *operands, log_total, mixed_t, grad_t)
    return outs


def join_kernel(
    kv, dq_ref, own_ref, one_ref, two_ref, cos_ref, sin_ref, wq_ref, wk_ref, wv_ref, *refs
):
    out_ref, keep_ref, send_ref, t_ref = refs
    wide = dq_ref.shape[0]
    cosine, sine = cos_ref[...], sin_ref[...]
    t_ref[:wide] = dq_ref[...].astype(F32)
    total = lambda i: own_ref[i] + sum(r[i].astype(F32) for r in (one_ref, two_ref))
    rotated_rows(t_ref.at[wide : wide + kv * HD], total(0), kv, cosine, -sine)
    t_ref[wide + kv * HD :] = total(1)
    out_ref[...] = t_ref[...].T.astype(BF)
    half = keep_ref.shape[0]
    parts = [
        (out_ref[:, :wide], wq_ref[0], 1),
        (t_ref[wide : wide + kv * HD].T.astype(BF), wk_ref[0], 0),
        (t_ref[wide + kv * HD :].T.astype(BF), wv_ref[0], 0),
    ]
    send_ref[...] = sum(mm(g[half:], w, 1, c) for g, w, c in parts).astype(BF)
    keep_ref[...] = sum(mm(g[:half], w, 1, c) for g, w, c in parts)


def join_call(dq, own, far, tables, weights, l, kv):
    rows = dq.shape[1]
    cols = dq.shape[0] + 2 * kv * HD
    width = weights[0].shape[1]
    whole = lambda v: pl.BlockSpec(v.shape, lambda i: (0,) * len(v.shape))
    outs = [
        jax.ShapeDtypeStruct((rows, cols), BF),
        jax.ShapeDtypeStruct((rows // 2, width), F32),
        jax.ShapeDtypeStruct((rows // 2, width), BF),
    ]
    given = (dq, own, *far, *tables)
    return pl.pallas_call(
        functools.partial(join_kernel, kv),
        grid=(1,),
        in_specs=[whole(v) for v in given] + [layer_block(w, l) for w in weights],
        out_specs=[whole(v) for v in outs],
        out_shape=outs,
        scratch_shapes=[pltpu.VMEM((cols, rows), F32)],
        compiler_params=pltpu.CompilerParams(vmem_limit_bytes=24 * MIB),
        name="join_gradients",
        cost_estimate=takes(5),
    )(*given, *weights)


def turned_halves(x, n):
    side = lax.axis_index("dp") % 2
    rows, cols = x.shape
    r, half = cols // n, cols // 2

    def kernel(side_ref, x_ref, mine_ref, other_ref, t_ref):
        t_ref[...] = x_ref[...].astype(F32).T.astype(BF)
        for odd in range(2):

            @pl.when(side_ref[0] == odd)
            def _():
                for b in range(n):
                    to = slice(b // 2 * r, (b // 2 + 1) * r)
                    block = t_ref[b * r : (b + 1) * r]
                    if b % 2 == odd:
                        mine_ref[to] = block
                    else:
                        other_ref[to] = block[:, : rows // 2]

    whole = pl.BlockSpec(memory_space=pltpu.VMEM)
    return pl.pallas_call(
        kernel,
        in_specs=[pl.BlockSpec(memory_space=pltpu.SMEM), whole],
        out_specs=[whole, whole],
        out_shape=[jax.ShapeDtypeStruct((half, rows), BF), jax.ShapeDtypeStruct((half, rows // 2), BF)],
        scratch_shapes=[pltpu.VMEM((cols, rows), BF)],
        compiler_params=pltpu.CompilerParams(vmem_limit_bytes=12 * MIB),
        name="turned_halves",
        cost_estimate=takes(3),
    )(side[None].astype(jnp.int32), x)


class Turned:
    def __init__(self, read, n):
        self.turn = Job(lambda token: turned_halves(after(read(), token), n))
        self.send = Job(lambda token: swap(after(self.turn.out[1], token), "dp", 1))
        self.whole = None

    def parts(self):
        if self.whole is None:
            got = self.send.out
            self.whole = jnp.concatenate([got, swap(got, "tensor", 1)], axis=1)
        return self.turn.out[0], self.whole


class Sent:
    def __init__(self, read, chunks):
        self.read = read
        self.sends = [self.chunk(i, chunks) for i in range(chunks)]

    def chunk(self, i, chunks):
        def make(token):
            x = self.read()
            rows = x.shape[0] // chunks
            return swap(after(x[i * rows : (i + 1) * rows], token), "dp", 1)

        return Job(make)

    def parts(self):
        got = [job.out for job in self.sends]
        return self.read(), got[0] if len(got) == 1 else jnp.concatenate(got, axis=0)


def product(left, right, cb=0):
    def make(token):
        (a, b), (c, d) = left.parts(), right.parts()
        return (mm(a, after(c, token), 1, cb) + mm(b, after(d, token), 1, cb)).astype(BF)

    return Job(make)


def joined(*products):
    def make(token):
        return jnp.concatenate([p.make(token) if p.raw is None else p.raw for p in products], axis=1)

    return Job(make)


def scatter(before, grad):
    return Job(lambda token: scatter_grad(after(grad.raw, None if before is None else before.raw)))


def inverse_rms(x):
    return lax.rsqrt(jnp.mean(x * x, axis=1, keepdims=True) + EPS)


def norm_back(x, inverse, gain, grad, incoming):
    normalized = x * inverse
    scaled = grad * gain
    gain_grad = jnp.sum(grad * normalized, axis=0)
    out = incoming + inverse * (
        scaled - normalized * jnp.mean(scaled * normalized, axis=1, keepdims=True)
    )
    return out, gain_grad


def shards(
    hidden_in,
    doc_lengths,
    norm_attn,
    norm_mlp,
    w_query,
    w_key,
    w_value,
    w_out,
    w_gate,
    w_up,
    w_down,
    cotangent,
):
    rows = hidden_in.shape[0]
    n = lax.axis_size("dp")
    quarter = rows // 4
    pair = rows // 2
    t = lax.axis_index("tensor")
    kv = w_key.shape[2] // HD
    heads = w_query.shape[2] // HD
    seq_count = n // STRETCHES
    shifted = lax.axis_index("dp") + STRETCHES // 2
    stretch = shifted % STRETCHES
    lengths = lax.dynamic_index_in_dim(doc_lengths, shifted // STRETCHES % seq_count, 0, keepdims=False)
    local = jnp.concatenate([(t ^ m) * quarter + jnp.arange(quarter, dtype=jnp.int32) for m in RELATIVE])
    place = stretch * rows + local
    ends = jnp.cumsum(lengths)
    passed = (place[:, None] >= ends[None, :]).astype(jnp.int32)
    start = jnp.sum(passed * lengths[None, :], axis=1)
    frequency = BASE ** (-(jnp.arange(HD // 2, dtype=F32) * 2.0 / HD))
    angles = frequency[:, None] * (place - start).astype(F32)[None, :]
    tables = (jnp.cos(angles), jnp.sin(angles))
    bases = jnp.stack([stretch, stretch ^ 1, stretch - 2, (stretch ^ 1) - 2]) * rows
    places = (bases.astype(jnp.int32), local[:, None], place[None, :], start[None, :])

    w_qkv = (w_query, jnp.swapaxes(w_key, 1, 2), jnp.swapaxes(w_value, 1, 2))

    def own_rows(x):
        return lax.dynamic_slice_in_dim(x, t * quarter, quarter, 0)

    value = {}

    def later(name, l):
        return lambda: value[name, l]

    layers = range(LAYERS)
    down_left = [Turned(later("down_in", l), n) for l in layers]
    attn_left = [Turned(later("normed", l), n) for l in layers]
    mlp_left = [Turned(later("normed_mlp", l), n) for l in layers]
    out_left = [Turned(later("out_in", l), n) for l in layers]
    act_right = [Sent(later("act", l), 2) for l in layers]
    mixed_right = [Sent(later("mixed", l), 1) for l in layers]
    gate_right = [Sent(later("gate", l), 2) for l in layers]
    up_right = [Sent(later("up", l), 2) for l in layers]
    qkv_right = [Sent(later("d_qkv", l), 2) for l in layers]
    g_down = [product(down_left[l], act_right[l]) for l in layers]
    g_gate = [product(mlp_left[l], gate_right[l]) for l in layers]
    g_up = [product(mlp_left[l], up_right[l]) for l in layers]
    g_out = [product(out_left[l], mixed_right[l], 1) for l in layers]
    g_qkv = [product(attn_left[l], qkv_right[l]) for l in layers]
    g_both = joined(g_gate[0], g_up[0])
    g_more = joined(g_up[1], g_down[1])
    g_attn = joined(g_out[1], g_qkv[1])
    s_gate = scatter(None, g_gate[1])
    s_more = scatter(s_gate, g_more)
    s_attn = scatter(s_more, g_attn)
    s_both = scatter(s_attn, g_both)
    g_tail = joined(g_out[0], g_qkv[0], g_down[0])
    s_tail = scatter(s_both, g_tail)
    plan = {
        ("keys", 0): [down_left[1].turn],
        ("attn", 0): [down_left[1].send],
        ("sum1", 0): [attn_left[0].turn, *mixed_right[0].sends],
        ("all1", 0): [attn_left[0].send],
        ("sum2", 0): [act_right[0].sends[0], mlp_left[0].turn],
        ("all2", 0): [act_right[0].sends[1]],
        ("attn", 1): [mlp_left[0].send],
        ("sum1", 1): [attn_left[1].turn, *mixed_right[1].sends],
        ("all1", 1): [attn_left[1].send],
        ("back_sum1", 1): [gate_right[1].sends[0], mlp_left[1].turn],
        ("back_all1", 1): [gate_right[1].sends[1]],
        ("back_attn", 1): [mlp_left[1].send, up_right[1].sends[0]],
        ("back_hop", 1): [out_left[1].turn],
        ("back_keys", 1): [up_right[1].sends[1], g_gate[1]],
        ("back_join", 1): [act_right[1].sends[0]],
        ("back_sum2", 1): [act_right[1].sends[1], g_up[1]],
        ("back_all2", 1): [out_left[1].send, g_more],
        ("back_mlp", 0): [qkv_right[1].sends[0], s_gate],
        ("back_sum1", 0): [qkv_right[1].sends[1], gate_right[0].sends[0], down_left[0].turn],
        ("back_all1", 0): [gate_right[0].sends[1], g_attn, s_more],
        ("back_attn", 0): [*up_right[0].sends],
        ("back_hop", 0): [g_gate[0], out_left[0].turn],
        ("back_keys", 0): [down_left[0].send, g_both, s_attn],
        ("back_join", 0): [out_left[0].send],
        ("back_sum2", 0): [*qkv_right[0].sends, g_down[0]],
        ("back_all2", 0): [g_tail],
    }
    jobs = lambda name, l: plan.get((name, l), [])

    value["down_in", LAYERS - 1] = to_relative(cotangent.astype(BF), t)
    flow = own_rows(hidden_in)
    inverse = inverse_rms(flow)
    normed_all = to_relative((hidden_in * inverse_rms(hidden_in) * norm_attn[0]).astype(BF), t)
    records = []
    for l in layers:
        value["normed", l] = normed_all
        q_t, kv_t = qkv_call(normed_all, w_qkv, l, tables, heads, kv)
        beside, behind, across = keys_onward(kv_t)
        across = window(kv_t, across, jobs("keys", l))
        blocks = (kv_t, beside, behind, across)
        mixed_t, log_total = attn_fwd(q_t, blocks, places, kv)
        mixed_t = value["mixed", l] = window(across, mixed_t, jobs("attn", l))
        send = mm(mixed_t[:, pair:], w_out[l], 0, 0).astype(BF)
        keep = mm(mixed_t[:, :pair], w_out[l], 0, 0)
        middle = flow + reduce_rows(keep, send, jobs("sum1", l))
        inverse_mlp = inverse_rms(middle)
        normed_mlp = gather_rows((middle * inverse_mlp * norm_mlp[l]).astype(BF), jobs("all1", l))
        value["normed_mlp", l] = normed_mlp
        gate, up, value["act", l], keep, send = mlp_call(normed_mlp, w_gate, w_up, w_down, l)
        send = window(normed_mlp, send, jobs("mlp", l))
        records.append((flow, inverse, q_t, blocks, log_total, middle, inverse_mlp, gate, up))
        if l + 1 < LAYERS:
            flow = middle + reduce_rows(keep, send, jobs("sum2", l))
            inverse = inverse_rms(flow)
            normed_all = gather_rows((flow * inverse * norm_attn[l + 1]).astype(BF), jobs("all2", l))

    def output_of(token):
        out = bf16_of(middle_last + reduce_rows(keep_last, after(send_last, token)))
        return to_absolute(gather_rows(out), t).astype(F32)

    middle_last, keep_last, send_last = middle, keep, send

    flow = own_rows(cotangent)
    gains = [None] * LAYERS
    for l in reversed(layers):
        before, inverse, q_t, blocks, log_total, middle, inverse_mlp, gate, up = records[l]
        down_in = value["down_in", l]
        gate_grad, up_grad, keep, send = mlp_back_call(down_in, w_down, w_gate, w_up, gate, up, l)
        value["gate", l], value["up", l] = gate_grad, up_grad
        send = window(down_in, send, jobs("back_mlp", l))
        total = reduce_rows(keep, send, jobs("back_sum1", l))
        flow, gain_mlp = norm_back(middle, inverse_mlp, norm_mlp[l], total, flow)
        out_in = value["out_in", l] = gather_rows(flow.astype(BF), jobs("back_all1", l))
        grad_t = mm(w_out[l], out_in, 1, 1).astype(BF)
        dq, own, *d_far = attn_bwd(q_t, blocks, places, kv, tables, log_total, value["mixed", l], grad_t)
        dq, d_far = window(out_in, (dq, d_far), jobs("back_attn", l))
        total, *d_far = keys_back(*d_far, jobs("back_hop", l))
        d_far = window(total, d_far, jobs("back_keys", l))
        d_qkv, keep, send = join_call(dq, own, d_far, tables, w_qkv, l, kv)
        value["d_qkv", l] = d_qkv
        send = window(d_far[1], send, jobs("back_join", l))
        if l + 1 == LAYERS:
            send, hidden_out = need(send, output_of(out_in))
        total = reduce_rows(keep, send, jobs("back_sum2", l))
        flow, gain_attn = norm_back(before, inverse, norm_attn[l], total, flow)
        gains[l] = (gain_attn, gain_mlp)
        if l > 0:
            value["down_in", l - 1] = gather_rows(flow.astype(BF), jobs("back_all2", l))
    final = gather_rows(bf16_of(flow), jobs("back_all2", 0))
    for job in (s_both, s_tail):
        job.out = job.raw = job.make(None)
    input_grad = to_absolute(final, t).astype(F32)

    gain_grads = jnp.stack([gains[0][0], gains[1][0], gains[0][1], gains[1][1]])
    gain_grads = sum_everywhere(after(gain_grads, g_tail.raw))
    width = gain_grads.shape[1] // n
    gain_grads = lax.dynamic_slice_in_dim(gain_grads, lax.axis_index("dp") * width, width, 1)
    norm_attn_grad, norm_mlp_grad = gain_grads[:LAYERS], gain_grads[LAYERS:]

    def stack(parts, turn=False):
        return jnp.stack([p.T if turn else p for p in parts])

    units = w_gate.shape[2]
    a, b, c = heads * HD, 2 * heads * HD, (2 * heads + kv) * HD
    d = c + kv * HD
    early = (
        hidden_out,
        input_grad,
        norm_attn_grad,
        norm_mlp_grad,
        stack([s_both.out[:, :units], s_gate.out]),
        stack([s_both.out[:, units:], s_more.out[:, :units]]),
    )
    *early, s_tail.out = need(*early, s_tail.out)
    attn = lambda start, stop: [job.out[:, start:stop] for job in (s_tail, s_attn)]
    return (
        *early[:4],
        stack(attn(a, b)),
        stack(attn(b, c)),
        stack(attn(c, d)),
        stack(attn(0, a), True),
        *early[4:],
        stack([s_tail.out[:, d:], s_more.out[:, units:]], True),
    )


def solution(mesh):
    placed = (
        P("dp", None),
        P(),
        P(),
        P(),
        P(None, None, "tensor"),
        P(None, None, "tensor"),
        P(None, None, "tensor"),
        P(None, "tensor", None),
        P(None, None, "tensor"),
        P(None, None, "tensor"),
        P(None, "tensor", None),
        P("dp", None),
    )
    return jax.shard_map(
        shards,
        mesh=mesh,
        in_specs=placed,
        out_specs=(
            P("dp", None),
            P("dp", None),
            P(None, "dp"),
            P(None, "dp"),
            P(None, "dp", "tensor"),
            P(None, "dp", "tensor"),
            P(None, "dp", "tensor"),
            P(None, "tensor", "dp"),
            P(None, "dp", "tensor"),
            P(None, "dp", "tensor"),
            P(None, "tensor", "dp"),
        ),
        check_vma=False,
    )
```

```python
import functools

import jax
import jax.numpy as jnp
from jax import lax
from jax.experimental import pallas as pl
from jax.experimental.pallas import tpu as pltpu
from jax.sharding import PartitionSpec as P

HD = 96
LAYERS = 2
STRETCHES = 4
EPS = 1e-05
BASE = 100000.0

BF = jnp.bfloat16
F32 = jnp.float32
NEG = -1e30
MIB = 2**20


def takes(us):
    return pl.CostEstimate(flops=int(us * 1.1e9), transcendentals=0, bytes_accessed=int(us * 1e6))


def mm(a, b, ca, cb):
    return lax.dot_general(a, b, (((ca,), (cb,)), ((), ())), preferred_element_type=F32)


def after(x, token):
    if token is None:
        return x
    return lax.optimization_barrier((x, token))[0]


def need(*values):
    return lax.optimization_barrier(values)


class Job:
    def __init__(self, make):
        self.make = make
        self.out = None
        self.raw = None


def window(start, end, jobs):
    if not jobs:
        return end
    for job in jobs:
        job.raw = job.make(start)
    leaves, tree = jax.tree.flatten((end, [job.raw for job in jobs]))
    end, outs = jax.tree.unflatten(tree, need(*leaves))
    for job, out in zip(jobs, outs):
        job.out = out
    return end


def swap(block, axis, mask):
    n = lax.axis_size(axis)
    return lax.ppermute(block, axis, [(i, i ^ mask) for i in range(n)])


def bf16_of(x):
    return lax.reduce_precision(x, 8, 7).astype(BF)


def gather_rows(own, jobs=()):
    beside = window(own, swap(own, "tensor", 2), jobs)
    pair = jnp.concatenate([own, beside], axis=0)
    return jnp.concatenate([pair, swap(pair, "tensor", 1)], axis=0)


def reduce_rows(keep, send, jobs=()):
    quarter = keep.shape[0] // 2
    got = swap(send, "tensor", 1)
    far = (keep[quarter:] + got[quarter:].astype(F32)).astype(BF)
    near = keep[:quarter] + got[:quarter].astype(F32)
    return near + window(far, swap(far, "tensor", 2), jobs).astype(F32)


RELATIVE = (0, 2, 1, 3)


def to_relative(rows, index):
    quarter = rows.shape[0] // 4
    return jnp.concatenate(
        [lax.dynamic_slice_in_dim(rows, (index ^ m) * quarter, quarter, 0) for m in RELATIVE], axis=0
    )


def to_absolute(rows, index):
    quarter = rows.shape[0] // 4
    parts = []
    for j in range(4):
        m = index ^ j
        place = ((m & 1) << 1) | (m >> 1)
        parts.append(lax.dynamic_slice_in_dim(rows, place * quarter, quarter, 0))
    return jnp.concatenate(parts, axis=0)


def in_stretches(pairs_of, n):
    pairs = []
    for i in range(n):
        offset = pairs_of((i + STRETCHES // 2) % STRETCHES)
        if offset is not None:
            pairs.append((i, (i + offset) % n))
    return pairs


def keys_onward(kv):
    n = lax.axis_size("dp")
    across = lax.ppermute(kv, "dp", in_stretches(lambda s: (3, 1, None, None)[s], n))
    behind = lax.ppermute(kv, "dp", in_stretches(lambda s: (2, 2, None, None)[s], n))
    return swap(kv, "dp", 1), behind, across


def keys_back(beside, behind, across, jobs):
    n = lax.axis_size("dp")
    late = [i for i in range(n) if (i + STRETCHES // 2) % STRETCHES >= 2]
    across = window(across, lax.ppermute(across, "dp", [(i, i ^ 1) for i in late]), jobs)
    total = (behind.astype(F32) + across.astype(F32)).astype(BF)
    back = in_stretches(lambda s: (None, None, -2, -2)[s], n)
    return total, swap(beside, "dp", 1), lax.ppermute(total, "dp", back)


def scatter_grad(grad):
    n = lax.axis_size("dp")
    groups = [list(range(side, n, 2)) for side in range(2)]
    out = lax.psum_scatter(
        grad.astype(BF), "dp", scatter_dimension=0, tiled=True, axis_index_groups=groups
    )
    return out.astype(F32)


def sum_everywhere(x):
    x = x + swap(x, "tensor", 1)
    x = x + swap(x, "tensor", 2)
    n = lax.axis_size("dp")
    mask = 1
    while mask < n:
        x = x + swap(x, "dp", mask)
        mask *= 2
    return x


def turned_pair(top, low, cosine, sine):
    return top * cosine - low * sine, low * cosine + top * sine


def layer_block(w, l):
    return pl.BlockSpec((1, *w.shape[1:]), lambda *_: (l, 0, 0))


WHOLE = pl.BlockSpec(memory_space=pltpu.VMEM)


def rotated_rows(out_ref, t, heads, cosine, sine):
    half = HD // 2
    for h in range(heads):
        a = h * HD
        top, low = turned_pair(t[a : a + half], t[a + half : a + HD], cosine, sine)
        out_ref[a : a + half] = top.astype(out_ref.dtype)
        out_ref[a + half : a + HD] = low.astype(out_ref.dtype)


def qkv_kernel(heads, kv, x_ref, wq_ref, wk_ref, wv_ref, cos_ref, sin_ref, q_ref, kv_ref):
    x = x_ref[...]
    cosine, sine = cos_ref[...], sin_ref[...]
    rotated_rows(q_ref, mm(x, wq_ref[0], 1, 0).T, heads, cosine, sine)
    rotated_rows(kv_ref, mm(wk_ref[0], x, 1, 1), kv, cosine, sine)
    kv_ref[kv * HD :] = mm(wv_ref[0], x, 1, 1).astype(BF)


def qkv_call(x, weights, l, tables, heads, kv):
    rows = x.shape[0]
    whole = lambda v: pl.BlockSpec(v.shape, lambda i: (0,) * v.ndim)
    outs = [jax.ShapeDtypeStruct((count * HD, rows), BF) for count in (heads, 2 * kv)]
    return pl.pallas_call(
        functools.partial(qkv_kernel, heads, kv),
        grid=(1,),
        in_specs=[whole(x), *(layer_block(w, l) for w in weights), *(whole(v) for v in tables)],
        out_specs=[whole(v) for v in outs],
        out_shape=outs,
        compiler_params=pltpu.CompilerParams(vmem_limit_bytes=20 * MIB),
        name="qkv_rotary",
        cost_estimate=takes(4.5),
    )(x, *weights, *tables)


def mlp_kernel(x_ref, wg_ref, wu_ref, wd_ref, gate_ref, up_ref, act_ref, keep_ref, send_ref, acc_ref):
    j = pl.program_id(0)
    x = x_ref[...]
    gate, up = mm(x, wg_ref[0], 1, 0), mm(x, wu_ref[0], 1, 0)
    gate_ref[...] = gate
    up_ref[...] = up
    act = (jax.nn.silu(gate) * up).astype(BF)
    act_ref[...] = act
    part = mm(act, wd_ref[0], 1, 0)

    @pl.when(j == 0)
    def _():
        acc_ref[...] = part

    @pl.when(j > 0)
    def _():
        acc_ref[...] += part

    split_sum(j, acc_ref, keep_ref, send_ref)


def split_sum(j, acc_ref, keep_ref, send_ref):
    @pl.when(j == pl.num_programs(0) - 1)
    def _():
        half = keep_ref.shape[0]
        keep_ref[...] = acc_ref[:half]
        send_ref[...] = acc_ref[half:].astype(BF)


UNITS = 512


def mlp_specs(x, l):
    rows, width = x.shape
    whole = lambda shape: pl.BlockSpec(shape, lambda j: (0, 0))
    wide = pl.BlockSpec((1, width, UNITS), lambda j: (l, 0, j))
    tall = pl.BlockSpec((1, UNITS, width), lambda j: (l, j, 0))
    part = pl.BlockSpec((rows, UNITS), lambda j: (0, j))
    sums = [whole((rows // 2, width))] * 2
    sum_shapes = [jax.ShapeDtypeStruct((rows // 2, width), F32), jax.ShapeDtypeStruct((rows // 2, width), BF)]
    return whole((rows, width)), wide, tall, part, sums, sum_shapes


def mlp_call(x, w_gate, w_up, w_down, l):
    whole, wide, tall, part, sums, sum_shapes = mlp_specs(x, l)
    shape = (x.shape[0], w_gate.shape[2])
    return pl.pallas_call(
        mlp_kernel,
        grid=(w_gate.shape[2] // UNITS,),
        in_specs=[whole, wide, wide, tall],
        out_specs=[part, part, part, *sums],
        out_shape=[jax.ShapeDtypeStruct(shape, d) for d in (F32, F32, BF)] + sum_shapes,
        scratch_shapes=[pltpu.VMEM(x.shape, F32)],
        compiler_params=pltpu.CompilerParams(vmem_limit_bytes=30 * MIB),
        name="feed_forward",
        cost_estimate=takes(8),
    )(x, w_gate, w_up, w_down)


def mlp_back_kernel(x_ref, wd_ref, wg_ref, wu_ref, gate_ref, up_ref, gg_ref, ug_ref, keep_ref, send_ref, acc_ref):
    j = pl.program_id(0)
    hidden = mm(x_ref[...], wd_ref[0], 1, 1)
    gate = gate_ref[...]
    sig = jax.nn.sigmoid(gate)
    gg = (hidden * up_ref[...] * sig * (1.0 + gate * (1.0 - sig))).astype(BF)
    ug = (hidden * gate * sig).astype(BF)
    gg_ref[...] = gg
    ug_ref[...] = ug
    part = mm(gg, wg_ref[0], 1, 1) + mm(ug, wu_ref[0], 1, 1)

    @pl.when(j == 0)
    def _():
        acc_ref[...] = part

    @pl.when(j > 0)
    def _():
        acc_ref[...] += part

    split_sum(j, acc_ref, keep_ref, send_ref)


def mlp_back_call(x, w_down, w_gate, w_up, gate, up, l):
    whole, wide, tall, part, sums, sum_shapes = mlp_specs(x, l)
    return pl.pallas_call(
        mlp_back_kernel,
        grid=(w_gate.shape[2] // UNITS,),
        in_specs=[whole, tall, wide, wide, part, part],
        out_specs=[part, part, *sums],
        out_shape=[jax.ShapeDtypeStruct(gate.shape, BF)] * 2 + sum_shapes,
        scratch_shapes=[pltpu.VMEM(x.shape, F32)],
        compiler_params=pltpu.CompilerParams(vmem_limit_bytes=30 * MIB),
        name="feed_forward_back",
        cost_estimate=takes(9),
    )(x, w_down, w_gate, w_up, gate, up)


def both_heads(block):
    return jnp.concatenate([block[:HD], block[HD:]], axis=1)


def flip(block):
    return block.astype(F32).T.astype(BF)


LOG2E = 1.4426950408889634


def fill_bias(base_ref, rows_ref, top_ref, start_ref, bias_ref):
    @pl.when(pl.program_id(0) == 0)
    def _():
        for b in range(4):
            place = rows_ref[...] + base_ref[b]
            allowed = (place >= start_ref[...]) & (place <= top_ref[...])
            bias_ref[b] = jnp.where(allowed, 0.0, NEG)


def scores_of(key, qt, bias):
    return mm(flip(key), qt, 1, 0) * (HD ** (-0.5) * LOG2E) + jnp.concatenate([bias, bias], axis=1)


def attn_fwd_kernel(base_ref, rows_ref, top_ref, start_ref, q_ref, *refs):
    keys, values = refs[0:8:2], refs[1:8:2]
    mixed_t_ref, log_ref, s_ref, bias_ref = refs[8:]
    fill_bias(base_ref, rows_ref, top_ref, start_ref, bias_ref)
    qt = both_heads(q_ref[...])
    top = jnp.full((1, qt.shape[1]), NEG, F32)
    for b in range(4):
        scores = scores_of(keys[b][...], qt, bias_ref[b])
        s_ref[b] = scores
        top = jnp.maximum(top, jnp.max(scores, axis=0, keepdims=True))
    total = jnp.zeros_like(top)
    acc = jnp.zeros((HD, qt.shape[1]), F32)
    for b in range(4):
        weight = jnp.exp2(s_ref[b] - top)
        total = total + jnp.sum(weight, axis=0, keepdims=True)
        acc = acc + mm(values[b][...], weight.astype(BF), 1, 0)
    acc = acc / total
    log_ref[0] = top + jnp.log(total) * LOG2E
    half = qt.shape[1] // 2
    mixed_t_ref[:HD] = acc[:, :half].astype(BF)
    mixed_t_ref[HD:] = acc[:, half:].astype(BF)


def attn_specs(rows, kv):
    q_spec = pl.BlockSpec((2 * HD, rows), lambda g: (g, 0))
    far_k = pl.BlockSpec((HD, rows), lambda g: (g, 0))
    far_v = pl.BlockSpec((HD, rows), lambda g: (kv + g, 0))
    whole = lambda shape: pl.BlockSpec(shape, lambda g: (0,) * len(shape))
    places = [
        pl.BlockSpec(memory_space=pltpu.SMEM),
        whole((rows, 1)),
        whole((1, rows)),
        whole((1, rows)),
    ]
    return places, q_spec, [far_k, far_v] * 4


def attn_fwd(q_t, blocks, places, kv):
    rows = q_t.shape[1]
    place_specs, q_spec, kv_specs = attn_specs(rows, kv)
    operands = [block for block in blocks for _ in range(2)]
    mixed_t, log_total = pl.pallas_call(
        attn_fwd_kernel,
        grid=(kv,),
        in_specs=place_specs + [q_spec] + kv_specs,
        out_specs=[
            pl.BlockSpec((2 * HD, rows), lambda g: (g, 0)),
            pl.BlockSpec((1, 1, 2 * rows), lambda g: (g, 0, 0)),
        ],
        out_shape=[
            jax.ShapeDtypeStruct((2 * kv * HD, rows), BF),
            jax.ShapeDtypeStruct((kv, 1, 2 * rows), F32),
        ],
        scratch_shapes=[pltpu.VMEM((4, rows, 2 * rows), F32), pltpu.VMEM((4, rows, rows), F32)],
        compiler_params=pltpu.CompilerParams(vmem_limit_bytes=24 * MIB),
        name="attention_forward",
        cost_estimate=takes(11),
    )(*places, q_t, *operands)
    return mixed_t, log_total


def attn_bwd_kernel(base_ref, rows_ref, top_ref, start_ref, cos_ref, sin_ref, q_ref, *refs):
    keys, values = refs[0:8:2], refs[1:8:2]
    log_ref, mixed_ref, grad_ref = refs[8:11]
    dq_ref, own_ref, bias_ref = refs[11], refs[12], refs[16]
    far_refs = refs[13:16]
    fill_bias(base_ref, rows_ref, top_ref, start_ref, bias_ref)
    qt = both_heads(q_ref[...])
    grad_t = both_heads(grad_ref[...])
    q_rows, grad_rows = flip(qt), flip(grad_t)
    log_total = log_ref[0]
    centre = jnp.sum(
        grad_t.astype(F32) * both_heads(mixed_ref[...]).astype(F32), axis=0, keepdims=True
    )
    dq = jnp.zeros((HD, qt.shape[1]), F32)
    for b in range(4):
        probs = jnp.exp2(scores_of(keys[b][...], qt, bias_ref[b]) - log_total)
        prob_grad = mm(flip(values[b][...]), grad_t, 1, 0)
        score_grad = (probs * (prob_grad - centre)).astype(BF)
        dq = dq + mm(keys[b][...], score_grad, 1, 0)
        dv = mm(probs.astype(BF), grad_rows, 1, 0).T
        dk = mm(score_grad, q_rows, 1, 0).T * HD ** (-0.5)
        out = own_ref if b == 0 else far_refs[b - 1]
        out[0] = dk.astype(out.dtype)
        out[1] = dv.astype(out.dtype)
    dq = dq * HD ** (-0.5)
    half, rows = HD // 2, qt.shape[1] // 2
    cosine, sine = cos_ref[...], sin_ref[...]
    for h in range(2):
        part = dq[:, h * rows : (h + 1) * rows]
        top, low = turned_pair(part[:half], part[half:], cosine, -sine)
        dq_ref[h * HD : h * HD + half] = top.astype(BF)
        dq_ref[h * HD + half : (h + 1) * HD] = low.astype(BF)


def attn_bwd(q_t, blocks, places, kv, tables, log_total, mixed_t, grad_t):
    rows = q_t.shape[1]
    place_specs, q_spec, kv_specs = attn_specs(rows, kv)
    operands = [block for block in blocks for _ in range(2)]
    table = pl.BlockSpec((HD // 2, rows), lambda g: (0, 0))
    two = pl.BlockSpec((2 * HD, rows), lambda g: (g, 0))
    pair = pl.BlockSpec((2, HD, rows), lambda g: (0, g, 0))
    outs = pl.pallas_call(
        attn_bwd_kernel,
        grid=(kv,),
        in_specs=place_specs
        + [table, table, q_spec]
        + kv_specs
        + [pl.BlockSpec((1, 1, 2 * rows), lambda g: (g, 0, 0)), two, two],
        out_specs=[two, pair, pair, pair, pair],
        out_shape=[jax.ShapeDtypeStruct((2 * kv * HD, rows), BF)]
        + [jax.ShapeDtypeStruct((2, kv * HD, rows), F32)]
        + [jax.ShapeDtypeStruct((2, kv * HD, rows), BF)] * 3,
        scratch_shapes=[pltpu.VMEM((4, rows, rows), F32)],
        compiler_params=pltpu.CompilerParams(vmem_limit_bytes=24 * MIB),
        name="attention_backward",
        cost_estimate=takes(16.5),
    )(*places, *tables, q_t, *operands, log_total, mixed_t, grad_t)
    return outs


def join_kernel(
    kv, dq_ref, own_ref, one_ref, two_ref, cos_ref, sin_ref, wq_ref, wk_ref, wv_ref, *refs
):
    out_ref, keep_ref, send_ref, t_ref = refs
    wide = dq_ref.shape[0]
    cosine, sine = cos_ref[...], sin_ref[...]
    t_ref[:wide] = dq_ref[...].astype(F32)
    total = lambda i: own_ref[i] + sum(r[i].astype(F32) for r in (one_ref, two_ref))
    rotated_rows(t_ref.at[wide : wide + kv * HD], total(0), kv, cosine, -sine)
    t_ref[wide + kv * HD :] = total(1)
    out_ref[...] = t_ref[...].T.astype(BF)
    half = keep_ref.shape[0]
    parts = [
        (out_ref[:, :wide], wq_ref[0], 1),
        (t_ref[wide : wide + kv * HD].T.astype(BF), wk_ref[0], 0),
        (t_ref[wide + kv * HD :].T.astype(BF), wv_ref[0], 0),
    ]
    send_ref[...] = sum(mm(g[half:], w, 1, c) for g, w, c in parts).astype(BF)
    keep_ref[...] = sum(mm(g[:half], w, 1, c) for g, w, c in parts)


def join_call(dq, own, far, tables, weights, l, kv):
    rows = dq.shape[1]
    cols = dq.shape[0] + 2 * kv * HD
    width = weights[0].shape[1]
    whole = lambda v: pl.BlockSpec(v.shape, lambda i: (0,) * len(v.shape))
    outs = [
        jax.ShapeDtypeStruct((rows, cols), BF),
        jax.ShapeDtypeStruct((rows // 2, width), F32),
        jax.ShapeDtypeStruct((rows // 2, width), BF),
    ]
    given = (dq, own, *far, *tables)
    return pl.pallas_call(
        functools.partial(join_kernel, kv),
        grid=(1,),
        in_specs=[whole(v) for v in given] + [layer_block(w, l) for w in weights],
        out_specs=[whole(v) for v in outs],
        out_shape=outs,
        scratch_shapes=[pltpu.VMEM((cols, rows), F32)],
        compiler_params=pltpu.CompilerParams(vmem_limit_bytes=24 * MIB),
        name="join_gradients",
        cost_estimate=takes(5),
    )(*given, *weights)


def turned_halves(x, n):
    side = lax.axis_index("dp") % 2
    rows, cols = x.shape
    r, half = cols // n, cols // 2

    def kernel(side_ref, x_ref, mine_ref, other_ref, t_ref):
        t_ref[...] = x_ref[...].astype(F32).T.astype(BF)
        for odd in range(2):

            @pl.when(side_ref[0] == odd)
            def _():
                for b in range(n):
                    to = slice(b // 2 * r, (b // 2 + 1) * r)
                    block = t_ref[b * r : (b + 1) * r]
                    if b % 2 == odd:
                        mine_ref[to] = block
                    else:
                        other_ref[to] = block[:, : rows // 2]

    whole = pl.BlockSpec(memory_space=pltpu.VMEM)
    return pl.pallas_call(
        kernel,
        in_specs=[pl.BlockSpec(memory_space=pltpu.SMEM), whole],
        out_specs=[whole, whole],
        out_shape=[jax.ShapeDtypeStruct((half, rows), BF), jax.ShapeDtypeStruct((half, rows // 2), BF)],
        scratch_shapes=[pltpu.VMEM((cols, rows), BF)],
        compiler_params=pltpu.CompilerParams(vmem_limit_bytes=12 * MIB),
        name="turned_halves",
        cost_estimate=takes(3),
    )(side[None].astype(jnp.int32), x)


class Turned:
    def __init__(self, read, n):
        self.turn = Job(lambda token: turned_halves(after(read(), token), n))
        self.send = Job(lambda token: swap(after(self.turn.out[1], token), "dp", 1))
        self.whole = None

    def parts(self):
        if self.whole is None:
            got = self.send.out
            self.whole = jnp.concatenate([got, swap(got, "tensor", 1)], axis=1)
        return self.turn.out[0], self.whole


class Sent:
    def __init__(self, read, chunks):
        self.read = read
        self.sends = [self.chunk(i, chunks) for i in range(chunks)]

    def chunk(self, i, chunks):
        def make(token):
            x = self.read()
            rows = x.shape[0] // chunks
            return swap(after(x[i * rows : (i + 1) * rows], token), "dp", 1)

        return Job(make)

    def parts(self):
        got = [job.out for job in self.sends]
        return self.read(), got[0] if len(got) == 1 else jnp.concatenate(got, axis=0)


def product(left, right, cb=0):
    def make(token):
        (a, b), (c, d) = left.parts(), right.parts()
        return (mm(a, after(c, token), 1, cb) + mm(b, after(d, token), 1, cb)).astype(BF)

    return Job(make)


def joined(*products):
    def make(token):
        return jnp.concatenate([p.make(token) if p.raw is None else p.raw for p in products], axis=1)

    return Job(make)


def scatter(before, grad):
    return Job(lambda token: scatter_grad(after(grad.raw, None if before is None else before.raw)))


def inverse_rms(x):
    return lax.rsqrt(jnp.mean(x * x, axis=1, keepdims=True) + EPS)


def norm_back(x, inverse, gain, grad, incoming):
    normalized = x * inverse
    scaled = grad * gain
    gain_grad = jnp.sum(grad * normalized, axis=0)
    out = incoming + inverse * (
        scaled - normalized * jnp.mean(scaled * normalized, axis=1, keepdims=True)
    )
    return out, gain_grad


def shards(
    hidden_in,
    doc_lengths,
    norm_attn,
    norm_mlp,
    w_query,
    w_key,
    w_value,
    w_out,
    w_gate,
    w_up,
    w_down,
    cotangent,
):
    rows = hidden_in.shape[0]
    n = lax.axis_size("dp")
    quarter = rows // 4
    pair = rows // 2
    t = lax.axis_index("tensor")
    kv = w_key.shape[2] // HD
    heads = w_query.shape[2] // HD
    seq_count = n // STRETCHES
    shifted = lax.axis_index("dp") + STRETCHES // 2
    stretch = shifted % STRETCHES
    lengths = lax.dynamic_index_in_dim(doc_lengths, shifted // STRETCHES % seq_count, 0, keepdims=False)
    local = jnp.concatenate([(t ^ m) * quarter + jnp.arange(quarter, dtype=jnp.int32) for m in RELATIVE])
    place = stretch * rows + local
    ends = jnp.cumsum(lengths)
    passed = (place[:, None] >= ends[None, :]).astype(jnp.int32)
    start = jnp.sum(passed * lengths[None, :], axis=1)
    frequency = BASE ** (-(jnp.arange(HD // 2, dtype=F32) * 2.0 / HD))
    angles = frequency[:, None] * (place - start).astype(F32)[None, :]
    tables = (jnp.cos(angles), jnp.sin(angles))
    bases = jnp.stack([stretch, stretch ^ 1, stretch - 2, (stretch ^ 1) - 2]) * rows
    places = (bases.astype(jnp.int32), local[:, None], place[None, :], start[None, :])

    w_qkv = (w_query, jnp.swapaxes(w_key, 1, 2), jnp.swapaxes(w_value, 1, 2))

    def own_rows(x):
        return lax.dynamic_slice_in_dim(x, t * quarter, quarter, 0)

    value = {}

    def later(name, l):
        return lambda: value[name, l]

    layers = range(LAYERS)
    down_left = [Turned(later("down_in", l), n) for l in layers]
    attn_left = [Turned(later("normed", l), n) for l in layers]
    mlp_left = [Turned(later("normed_mlp", l), n) for l in layers]
    out_left = [Turned(later("out_in", l), n) for l in layers]
    act_right = [Sent(later("act", l), 2) for l in layers]
    mixed_right = [Sent(later("mixed", l), 1) for l in layers]
    gate_right = [Sent(later("gate", l), 2) for l in layers]
    up_right = [Sent(later("up", l), 4 - 2 * l) for l in layers]
    qkv_right = [Sent(later("d_qkv", l), 2) for l in layers]
    g_down = [product(down_left[l], act_right[l]) for l in layers]
    g_gate = [product(mlp_left[l], gate_right[l]) for l in layers]
    g_up = [product(mlp_left[l], up_right[l]) for l in layers]
    g_out = [product(out_left[l], mixed_right[l], 1) for l in layers]
    g_qkv = [product(attn_left[l], qkv_right[l]) for l in layers]
    g_both = joined(g_gate[0], g_up[0])
    g_more = joined(g_up[1], g_down[1])
    g_attn = joined(g_out[1], g_qkv[1])
    s_gate = scatter(None, g_gate[1])
    s_more = scatter(s_gate, g_more)
    s_attn = scatter(s_more, g_attn)
    s_both = scatter(s_attn, g_both)
    g_tail = joined(g_out[0], g_qkv[0], g_down[0])
    s_tail = scatter(s_both, g_tail)
    plan = {
        ("keys", 0): [down_left[1].turn],
        ("attn", 0): [down_left[1].send],
        ("sum1", 0): [attn_left[0].turn, *mixed_right[0].sends],
        ("all1", 0): [attn_left[0].send],
        ("sum2", 0): [act_right[0].sends[0], mlp_left[0].turn],
        ("all2", 0): [act_right[0].sends[1]],
        ("attn", 1): [mlp_left[0].send],
        ("sum1", 1): [attn_left[1].turn, *mixed_right[1].sends],
        ("all1", 1): [attn_left[1].send],
        ("back_sum1", 1): [gate_right[1].sends[0], mlp_left[1].turn],
        ("back_all1", 1): [gate_right[1].sends[1]],
        ("back_attn", 1): [mlp_left[1].send, up_right[1].sends[0]],
        ("back_hop", 1): [out_left[1].turn],
        ("back_keys", 1): [up_right[1].sends[1], g_gate[1]],
        ("back_join", 1): [act_right[1].sends[0]],
        ("back_sum2", 1): [act_right[1].sends[1], g_up[1]],
        ("back_all2", 1): [out_left[1].send, g_more],
        ("back_mlp", 0): [qkv_right[1].sends[0], s_gate],
        ("back_sum1", 0): [qkv_right[1].sends[1], gate_right[0].sends[0], down_left[0].turn],
        ("back_all1", 0): [gate_right[0].sends[1], up_right[0].sends[0], g_attn, s_more],
        ("back_attn", 0): up_right[0].sends[1:],
        ("back_hop", 0): [g_gate[0], out_left[0].turn],
        ("back_keys", 0): [down_left[0].send, g_both, s_attn],
        ("back_join", 0): [out_left[0].send],
        ("back_sum2", 0): [*qkv_right[0].sends, g_down[0]],
        ("back_all2", 0): [g_tail],
    }
    jobs = lambda name, l: plan.get((name, l), [])

    value["down_in", LAYERS - 1] = to_relative(cotangent.astype(BF), t)
    flow = own_rows(hidden_in)
    inverse = inverse_rms(flow)
    normed_all = to_relative((hidden_in * inverse_rms(hidden_in) * norm_attn[0]).astype(BF), t)
    records = []
    for l in layers:
        value["normed", l] = normed_all
        q_t, kv_t = qkv_call(normed_all, w_qkv, l, tables, heads, kv)
        beside, behind, across = keys_onward(kv_t)
        across = window(kv_t, across, jobs("keys", l))
        blocks = (kv_t, beside, behind, across)
        mixed_t, log_total = attn_fwd(q_t, blocks, places, kv)
        mixed_t = value["mixed", l] = window(across, mixed_t, jobs("attn", l))
        send = mm(mixed_t[:, pair:], w_out[l], 0, 0).astype(BF)
        keep = mm(mixed_t[:, :pair], w_out[l], 0, 0)
        middle = flow + reduce_rows(keep, send, jobs("sum1", l))
        inverse_mlp = inverse_rms(middle)
        normed_mlp = gather_rows((middle * inverse_mlp * norm_mlp[l]).astype(BF), jobs("all1", l))
        value["normed_mlp", l] = normed_mlp
        gate, up, value["act", l], keep, send = mlp_call(normed_mlp, w_gate, w_up, w_down, l)
        send = window(normed_mlp, send, jobs("mlp", l))
        records.append((flow, inverse, q_t, blocks, log_total, middle, inverse_mlp, gate, up))
        if l + 1 < LAYERS:
            flow = middle + reduce_rows(keep, send, jobs("sum2", l))
            inverse = inverse_rms(flow)
            normed_all = gather_rows((flow * inverse * norm_attn[l + 1]).astype(BF), jobs("all2", l))

    def output_of(token):
        out = bf16_of(middle_last + reduce_rows(keep_last, after(send_last, token)))
        return to_absolute(gather_rows(out), t).astype(F32)

    middle_last, keep_last, send_last = middle, keep, send

    flow = own_rows(cotangent)
    gains = [None] * LAYERS
    for l in reversed(layers):
        before, inverse, q_t, blocks, log_total, middle, inverse_mlp, gate, up = records[l]
        down_in = value["down_in", l]
        gate_grad, up_grad, keep, send = mlp_back_call(down_in, w_down, w_gate, w_up, gate, up, l)
        value["gate", l], value["up", l] = gate_grad, up_grad
        send = window(down_in, send, jobs("back_mlp", l))
        total = reduce_rows(keep, send, jobs("back_sum1", l))
        flow, gain_mlp = norm_back(middle, inverse_mlp, norm_mlp[l], total, flow)
        out_in = value["out_in", l] = gather_rows(flow.astype(BF), jobs("back_all1", l))
        grad_t = mm(w_out[l], out_in, 1, 1).astype(BF)
        dq, own, *d_far = attn_bwd(q_t, blocks, places, kv, tables, log_total, value["mixed", l], grad_t)
        dq, d_far = window(out_in, (dq, d_far), jobs("back_attn", l))
        total, *d_far = keys_back(*d_far, jobs("back_hop", l))
        d_far = window(total, d_far, jobs("back_keys", l))
        d_qkv, keep, send = join_call(dq, own, d_far, tables, w_qkv, l, kv)
        value["d_qkv", l] = d_qkv
        send = window(d_far[1], send, jobs("back_join", l))
        if l + 1 == LAYERS:
            send, hidden_out = need(send, output_of(out_in))
        total = reduce_rows(keep, send, jobs("back_sum2", l))
        flow, gain_attn = norm_back(before, inverse, norm_attn[l], total, flow)
        gains[l] = (gain_attn, gain_mlp)
        if l > 0:
            value["down_in", l - 1] = gather_rows(flow.astype(BF), jobs("back_all2", l))
    final = gather_rows(bf16_of(flow), jobs("back_all2", 0))
    for job in (s_both, s_tail):
        job.out = job.raw = job.make(None)
    input_grad = to_absolute(final, t).astype(F32)

    gain_grads = jnp.stack([gains[0][0], gains[1][0], gains[0][1], gains[1][1]])
    gain_grads = sum_everywhere(after(gain_grads, g_tail.raw))
    width = gain_grads.shape[1] // n
    gain_grads = lax.dynamic_slice_in_dim(gain_grads, lax.axis_index("dp") * width, width, 1)
    norm_attn_grad, norm_mlp_grad = gain_grads[:LAYERS], gain_grads[LAYERS:]

    def stack(parts, turn=False):
        return jnp.stack([p.T if turn else p for p in parts])

    units = w_gate.shape[2]
    a, b, c = heads * HD, 2 * heads * HD, (2 * heads + kv) * HD
    d = c + kv * HD
    early = (
        hidden_out,
        input_grad,
        norm_attn_grad,
        norm_mlp_grad,
        stack([s_both.out[:, :units], s_gate.out]),
        stack([s_both.out[:, units:], s_more.out[:, :units]]),
    )
    *early, s_tail.out = need(*early, s_tail.out)
    attn = lambda start, stop: [job.out[:, start:stop] for job in (s_tail, s_attn)]
    return (
        *early[:4],
        stack(attn(a, b)),
        stack(attn(b, c)),
        stack(attn(c, d)),
        stack(attn(0, a), True),
        *early[4:],
        stack([s_tail.out[:, d:], s_more.out[:, units:]], True),
    )


def solution(mesh):
    placed = (
        P("dp", None),
        P(),
        P(),
        P(),
        P(None, None, "tensor"),
        P(None, None, "tensor"),
        P(None, None, "tensor"),
        P(None, "tensor", None),
        P(None, None, "tensor"),
        P(None, None, "tensor"),
        P(None, "tensor", None),
        P("dp", None),
    )
    return jax.shard_map(
        shards,
        mesh=mesh,
        in_specs=placed,
        out_specs=(
            P("dp", None),
            P("dp", None),
            P(None, "dp"),
            P(None, "dp"),
            P(None, "dp", "tensor"),
            P(None, "dp", "tensor"),
            P(None, "dp", "tensor"),
            P(None, "tensor", "dp"),
            P(None, "dp", "tensor"),
            P(None, "dp", "tensor"),
            P(None, "tensor", "dp"),
        ),
        check_vma=False,
    )
```
